512 devices in a mesh: rows: 64 (over y, z), cols: 8 (over x, core).
Axes of the slice: x: 4, y: 4, z: 16, core: 2. Of those that a mesh axis runs over, the one named last changes fastest.
Arguments:
- images: float32 [512, 32, 128], P('rows'), may hold values from -6 to 6
- gauge_pixel: int32 [131072], P('rows'), may hold values from 0 to 32767
- row_mask: int32 [131072], P('rows'), may hold values 0 or 1
- gauge_counts: int32 [64], P('rows'), may hold values from 1 to 2048, as said below
- targets: float32 [131072], P('rows'), may hold values from -10 to 10
- theta: float32 [64, 8], replicated, may hold values from -2.5 to 2.5
- amplitude: float32 [64], replicated, may hold values from 0.5 to 1.5
- damping: float32 [], replicated, may hold values from 0.05 to 0.3
Outputs:
- r_factor: float32 [512, 512], replicated
- new_theta: float32 [64, 8], replicated
- predicted: float32 [131072], P(('rows', 'cols'))
The draws below stay inside these ranges and needn't reach their ends.
Inputs may be any that keep to these rules, and one draw needn't show every extreme that they name: The slots in use on an index of rows are its first gauge_counts slots; one index of rows uses all 2048.
All inputs are finite; a program needn't handle non-finite values. No bound on the sum of `row_mask` on one device may be relied on, other than what follows from the above.
Results may differ from the reference program's by a relative error of at most 0.0003.
Values sent between devices are 32-bit elements; how exact they have to be, the bound alone decides.
A program may use at most 64 MiB of HBM per device.

```python
import math
import jax
import jax.numpy as jnp
from jax import lax

CH = 64
KB = 8
TH = 32
TW = 128
CLIP_DEV = 8
G_CAP = 2048
PARAMS = 512
ROW_GROUPS = 64
CLIPS = 512
GAUGES = 131072


def draw_gauge_counts(key, part):
    first_key = jax.random.fold_in(key, 11)
    second_key = jax.random.fold_in(key, 23)
    device_rank = jnp.arange(ROW_GROUPS)
    baseline = G_CAP // 3 + (G_CAP - G_CAP // 3) * device_rank // max(ROW_GROUPS - 1, 1)
    shortfall = jax.random.randint(first_key, (ROW_GROUPS,), 0, G_CAP // 8 + 1)
    fullest = jax.random.randint(second_key, (), 0, ROW_GROUPS)
    counts = jnp.where(device_rank == fullest, G_CAP, baseline - shortfall)
    return counts.astype(jnp.int32)


def place_ends(values, key, low, high):
    index_at = [jax.random.randint(jax.random.fold_in(key, axis), (), 0, length) for axis, length in enumerate(values.shape)]
    longest = values.shape.index(max(values.shape))
    next_to = index_at[:longest] + [(index_at[longest] + 1) % values.shape[longest]] + index_at[longest + 1:]
    return values.at[tuple(index_at)].set(low).at[tuple(next_to)].set(high)


def block_levels(stream_key, shape, shards, smallest, largest):
    def one(position, shards_of):
        draws = jax.random.uniform(jax.random.fold_in(jax.random.fold_in(stream_key, 6), position), (shards_of,), jnp.float32, smallest / len(shards), largest / len(shards))
        return jnp.repeat(jnp.exp(draws), shape[position] // shards_of).reshape((-1,) + (1,) * (len(shape) - position - 1))

    factor_of = one(*shards[0])
    for cut in shards[1:]:
        factor_of = factor_of * one(*cut)
    return factor_of


def bell_draw(stream_key, dims, scale, bound, cuts=(), kind=jnp.bfloat16):
    entries = jax.random.normal(stream_key, dims, jnp.float32) * scale
    if len(cuts) > 0:
        entries = block_levels(stream_key, dims, cuts, -0.22, 0.18) * entries
    return jnp.clip(entries, min=-bound, max=bound).astype(kind)


def setup_inputs(seed: int = 0) -> dict:
    seeds = jax.random.split(jax.random.key(seed), 9)
    return {
        "images": bell_draw(seeds[0], (CLIPS, TH, TW), 1.0, 6.0, ((0, 64),), jnp.float32),
        "gauge_pixel": place_ends(jax.random.randint(seeds[1], (GAUGES,), 0, CLIP_DEV * TH * TW), jax.random.fold_in(seeds[1], 1), 0, (CLIP_DEV * TH * TW) - 1).astype(jnp.int32),
        "row_mask": place_ends((jax.random.randint(seeds[2], (GAUGES,), 0, 8) < 7).astype(jnp.int32), jax.random.fold_in(seeds[2], 1), 0, 1),
        "gauge_counts": draw_gauge_counts(jax.random.fold_in(seeds[8], 71), 0),
        "targets": bell_draw(seeds[4], (GAUGES,), 2.0, 10.0, ((0, 64),), jnp.float32),
        "theta": bell_draw(seeds[5], (CH, KB), 0.35, 2.5, (), jnp.float32),
        "amplitude": jnp.clip(jnp.exp(jax.random.uniform(seeds[6], (CH,), jnp.float32, math.log(0.5), math.log(1.5))), 0.5, 1.5),
        "damping": jnp.clip(jnp.exp(jax.random.uniform(seeds[7], (), jnp.float32, math.log(0.05), math.log(0.3))), 0.05, 0.3),
    }


y_orders = [0, 1, 0, 2, 1, 0, 0, 0]
x_orders = [0, 0, 1, 0, 1, 2, 0, 2]
sigmas = [1.5, 1.5, 1.5, 1.5, 1.5, 1.5, 3.0, 3.0]

def kernel_values(spacing, deriv_order, width_sigma):
    envelope = jnp.exp(-spacing * spacing / (2.0 * width_sigma * width_sigma))
    if deriv_order == 1:
        return -spacing / width_sigma ** 2 * envelope
    if deriv_order == 2:
        return (spacing * spacing / width_sigma ** 4 - 1.0 / width_sigma ** 2) * envelope
    return envelope

def kernel_table(length, deriv_order, width_sigma):
    places = jnp.arange(length)
    spacing = (places[:, None] - places[None, :]).astype(jnp.float32)
    sample = jnp.arange(-12, 13).astype(jnp.float32)
    scaling = jnp.sqrt(jnp.sum(kernel_values(sample, deriv_order, width_sigma) ** 2))
    return kernel_values(spacing, deriv_order, width_sigma) / scaling

def features(clip_tiles):
    height = clip_tiles.shape[1]
    breadth = clip_tiles.shape[2]
    left_tabs = jnp.stack([kernel_table(height, y_orders[which], sigmas[which]) for which in range(8)])
    right_tabs = jnp.stack([kernel_table(breadth, x_orders[which], sigmas[which]) for which in range(8)])
    partial_conv = jnp.einsum('kij,cjw->kciw', left_tabs, clip_tiles, precision=lax.Precision.HIGHEST)
    full_conv = jnp.einsum('kciw,kvw->kciv', partial_conv, right_tabs, precision=lax.Precision.HIGHEST)
    return full_conv.reshape(full_conv.shape[0], -1)

def group_terms(clip_tiles, pixels, valid, count, measured, theta, amplitude):
    slots = pixels.shape[0]
    live = ((jnp.arange(slots) < count) & (valid == 1)).astype(jnp.float32)
    flat_feats = features(clip_tiles)
    phi = jnp.take(flat_feats, pixels, axis=1).T
    act = jnp.tanh(jnp.dot(phi, theta.T, precision=lax.Precision.HIGHEST))
    model = jnp.dot(act, amplitude, precision=lax.Precision.HIGHEST)
    resid = live * (model - measured)
    slope = live[:, None] * amplitude[None, :] * (1.0 - act * act)
    jac = (slope[:, :, None] * phi[:, None, :]).reshape(slots, -1)
    return (jac, resid, live)

def solve_step(lower, rhs):
    inner = lax.linalg.triangular_solve(lower, rhs[:, None], left_side=True, lower=True)
    outer = lax.linalg.triangular_solve(lower, inner, left_side=True, lower=True, transpose_a=True)
    return -outer[:, 0]

def reference(images, gauge_pixel, row_mask, gauge_counts, targets, theta, amplitude, damping):
    tiles = images.reshape(ROW_GROUPS, CLIP_DEV, TH, TW)
    pixels = gauge_pixel.reshape(ROW_GROUPS, G_CAP)
    valid = row_mask.reshape(ROW_GROUPS, G_CAP)
    measured = targets.reshape(ROW_GROUPS, G_CAP)
    inputs = (tiles, pixels, valid, gauge_counts, measured)

    def accumulate(carry, group):
        jac, resid, live = group_terms(group[0], group[1], group[2], group[3], group[4], theta, amplitude)
        gram = carry[0] + jnp.dot(jac.T, jac, precision=lax.Precision.HIGHEST)
        grad = carry[1] + jnp.dot(jac.T, resid, precision=lax.Precision.HIGHEST)
        return ((gram, grad, carry[2] + jnp.sum(live)), None)
    start = (jnp.zeros((PARAMS, PARAMS), jnp.float32), jnp.zeros((PARAMS,), jnp.float32), jnp.zeros((), jnp.float32))
    sums, unused = lax.scan(accumulate, start, inputs)
    gram, grad, total = sums
    normal = gram / total + damping * jnp.eye(PARAMS, dtype=jnp.float32)
    lower = jnp.linalg.cholesky(normal)
    step = solve_step(lower, grad / total)

    def predict(carry, group):
        jac, resid, live = group_terms(group[0], group[1], group[2], group[3], group[4], theta, amplitude)
        return (carry, resid + jnp.dot(jac, step, precision=lax.Precision.HIGHEST))
    unused_carry, predicted = lax.scan(predict, jnp.zeros((), jnp.float32), inputs)
    return (lower.T, theta + step.reshape(CH, KB), predicted.reshape(GAUGES))
```

```python
import functools

import jax
import jax.numpy as jnp
import numpy as np
from jax import lax
from jax.experimental import pallas as pl
from jax.experimental.pallas import tpu as pltpu
from jax.sharding import PartitionSpec as P

HI = lax.Precision.HIGHEST
F32 = jnp.float32
NN = (((1,), (0,)), ((), ()))
NT = (((1,), (1,)), ((), ()))
TN = (((0,), (0,)), ((), ()))
MESH = pl.DeviceIdType.MESH

Y_KIND = [(0, 1.5), (1, 1.5), (0, 1.5), (2, 1.5), (1, 1.5), (0, 1.5), (0, 3.0), (0, 3.0)]
X_KIND = [(0, 1.5), (0, 1.5), (1, 1.5), (0, 1.5), (1, 1.5), (2, 1.5), (0, 3.0), (2, 3.0)]

NB = 128
PARAMS = 512
BLOCKS = [(i, j) for i in range(4) for j in range(i, 4)]
PLANE = 16
ZN = 16
ZROWS = 3
CHUNK = ZN * ZROWS
ROWS = 2 * PLANE * CHUNK
GRAD_ROW = len(BLOCKS) * NB


def dot(a, b, dims):
    return lax.dot_general(a, b, dims, precision=HI, preferred_element_type=F32)


def norm_of(order, width):
    t = np.arange(-12, 13).astype(np.float64)
    e = np.exp(-t * t / (2.0 * width * width))
    if order == 1:
        e = -t / width**2 * e
    if order == 2:
        e = (t * t / width**4 - 1.0 / width**2) * e
    return float(1.0 / np.sqrt(np.sum(e * e)))


def filters(t, kinds):
    t2 = t * t
    env = {w: jnp.exp(t2 * (-1.0 / (2.0 * w * w))) for w in sorted({w for _, w in kinds})}
    out = {}
    for order, w in sorted(set(kinds)):
        scale = norm_of(order, w)
        if order == 0:
            out[order, w] = env[w] * scale
        elif order == 1:
            out[order, w] = t * (-scale / w**2) * env[w]
        else:
            out[order, w] = (t2 * (scale / w**4) - scale / w**2) * env[w]
    return out


def iota(shape, dim):
    return lax.broadcasted_iota(jnp.int32, shape, dim)


def local_kernel(count_ref, img_ref, pix_ref, mask_ref, targ_ref, theta_ref, amp_ref,
                 packed_ref, slope_ref, phi_ref, resid_ref):
    col = lax.axis_index("cols")

    def own(ref):
        v = ref[pl.ds(2 * col, 2), :]
        return jnp.concatenate([v[0:1, :], v[1:2, :]], axis=1)

    pix = own(pix_ref)
    slots = pix.shape[1]
    place = col * slots + iota((1, slots), 1)
    live = ((place < count_ref[0]) & (own(mask_ref) == 1)).astype(F32)

    img = img_ref[...]
    src = iota((img.shape[0], slots), 0)
    row = pix >> 7
    near = (src >> 5) == (row >> 5)
    ty = ((row & 31) - (src & 31)).astype(F32)
    yk = filters(ty, Y_KIND)
    keys = sorted(yk)
    left = jnp.concatenate([jnp.where(near, yk[k], 0.0) for k in keys], axis=1)
    part = dot(img, left, TN)
    tx = ((pix & 127) - iota((img.shape[1], slots), 0)).astype(F32)
    xk = filters(tx, X_KIND)
    phis = []
    for ky, kx in zip(Y_KIND, X_KIND):
        at = keys.index(ky) * slots
        phis.append(jnp.sum(part[:, at:at + slots] * xk[kx], axis=0, keepdims=True))
    phi = jnp.concatenate(phis, axis=0)
    phi_ref[...] = phi

    act = jnp.tanh(dot(theta_ref[...], phi, NN))
    amp = amp_ref[...]
    resid = live * (jnp.sum(amp * act, axis=0, keepdims=True) - own(targ_ref))
    resid_ref[...] = resid
    slope = live * amp * (1.0 - act * act)
    slope_ref[...] = slope
    jac = jnp.concatenate([slope[c:c + 1, :] * phi for c in range(slope.shape[0])], axis=0)

    for i in range(4):
        wide = dot(jac[i * NB:(i + 1) * NB], jac[i * NB:], NT)
        for j in range(i, 4):
            at = BLOCKS.index((i, j)) * NB
            packed_ref[at:at + NB, :] = wide[:, (j - i) * NB:(j - i + 1) * NB]
    grad = dot(jnp.broadcast_to(resid, (8, slots)), jac, NT)
    total = jnp.sum(live, axis=1, keepdims=True)
    rows = [grad[0:1, i * NB:(i + 1) * NB] for i in range(4)]
    rows += [jnp.broadcast_to(total, (1, NB)), jnp.zeros((3, NB), F32)]
    packed_ref[GRAD_ROW:GRAD_ROW + 8, :] = jnp.concatenate(rows, axis=0)
    packed_ref[GRAD_ROW + 8:, :] = jnp.zeros((ROWS - GRAD_ROW - 8, NB), F32)


def reduce_kernel(ysize, x_ref, o_ref, got0, part, got1, zout, got2, zall, full,
                  s0, r0, s1, r1, s2, r2, s3, r3, s4, r4, s5, r5):
    row = lax.axis_index("rows")
    col = lax.axis_index("cols")
    y, z = row // ZN, lax.rem(row, ZN)
    x, core = col // 2, lax.rem(col, 2)
    me = x * ysize + y

    def at_plane(p):
        return {"rows": lax.rem(p, ysize) * ZN + z, "cols": (p // ysize) * 2 + core}

    def at_z(q):
        return {"rows": y * ZN + q, "cols": col}

    partner = {"rows": row, "cols": x * 2 + 1 - core}
    planes = [lax.rem(me + d, PLANE) for d in range(1, PLANE)]
    zs = [lax.rem(z + d, ZN) for d in range(1, ZN)]

    barrier = pltpu.get_barrier_semaphore()
    pl.semaphore_signal(barrier, inc=1, device_id=partner, device_id_type=MESH)
    for p in planes:
        pl.semaphore_signal(barrier, inc=1, device_id=at_plane(p), device_id_type=MESH)
    for q in zs:
        pl.semaphore_signal(barrier, inc=1, device_id=at_z(q), device_id_type=MESH)
    pl.semaphore_wait(barrier, 1 + 2 * 15)

    def copy(src, dst, ssem, rsem, dev):
        return pltpu.make_async_remote_copy(
            src_ref=src, dst_ref=dst, send_sem=ssem, recv_sem=rsem,
            device_id=dev, device_id_type=MESH)

    sends = []

    def start(c):
        c.start()
        sends.append(c)

    order = planes + [me]
    for p in order:
        start(copy(x_ref.at[1 - core, p], got0.at[p], s0.at[p], r0.at[p], partner))
    for d, p in enumerate(order):
        copy(x_ref.at[core, p], got0.at[p], s0.at[p], r0.at[p], partner).wait_recv()
        part[p] = x_ref[core, p] + got0[p]
        if d < PLANE - 1:
            start(copy(part.at[p], got1.at[me], s1.at[p], r1.at[me], at_plane(p)))
    acc = part[me]
    for p in planes:
        copy(part.at[p], got1.at[p], s1.at[p], r1.at[p], at_plane(p)).wait_recv()
        acc = acc + got1[p]
    for q in range(ZN):
        zout[q] = acc[q * ZROWS:(q + 1) * ZROWS, :]
    for q in zs:
        start(copy(zout.at[q], got2.at[z], s2.at[q], r2.at[z], at_z(q)))
    tot = zout[z]
    for q in zs:
        copy(zout.at[q], got2.at[q], s2.at[q], r2.at[q], at_z(q)).wait_recv()
        tot = tot + got2[q]
    zall[z] = tot
    for q in zs:
        start(copy(zall.at[z], zall.at[z], s3.at[q], r3.at[z], at_z(q)))
    for q in zs:
        copy(zall.at[q], zall.at[q], s3.at[q], r3.at[q], at_z(q)).wait_recv()
    full[core, me] = jnp.concatenate([zall[q] for q in range(ZN)], axis=0)
    for p in planes:
        start(copy(full.at[core, me], full.at[core, me], s4.at[p], r4.at[me], at_plane(p)))
    start(copy(full.at[core, me], full.at[core, me], s5.at[me], r5.at[me], partner))
    for p in planes:
        copy(full.at[core, p], full.at[core, p], s4.at[p], r4.at[p], at_plane(p)).wait_recv()
        start(copy(full.at[core, p], full.at[core, p], s5.at[p], r5.at[p], partner))
    for p in order:
        copy(full.at[1 - core, p], full.at[1 - core, p], s5.at[p], r5.at[p], partner).wait_recv()
    for c in sends:
        c.wait_send()
    o_ref[...] = full[...]


def lane(v, c):
    return jnp.broadcast_to(v[:, c:c + 1], (8, NB))


def sub(v, r):
    return jnp.broadcast_to(v[r:r + 1, :], (8, NB))


def factor_block(a, w):
    n = len(a)
    row8 = iota((8, NB), 0)
    col = iota((8, NB), 1)
    rs, ws = [], []

    def stack(rows):
        out = rows[0]
        for i in range(1, 8):
            out = jnp.where(row8 == i, rows[i], out)
        return out

    for s in range(n):
        base = 8 * s
        cb = [lane(a[s], base + m) for m in range(8)]
        t = [[sub(cb[m], i) if i >= m else None for m in range(8)] for i in range(8)]
        pa = [sub(a[s], i) for i in range(8)]
        pw = [sub(w[s], i) for i in range(8)]
        nxt = [lane(a[s + 1], base + m) for m in range(8)] if s + 1 < n else None
        nx = list(nxt) if nxt is not None else None
        low = [[None] * 8 for _ in range(8)]
        inv = []
        for j in range(8):
            r = lax.rsqrt(t[j][j])
            inv.append(r)
            for i in range(j + 1, 8):
                low[i][j] = t[i][j] * r
            pa[j] = pa[j] * r
            pw[j] = pw[j] * r
            if nx is not None:
                nx[j] = nx[j] * r
            for i in range(j + 1, 8):
                for m in range(j + 1, i + 1):
                    t[i][m] = t[i][m] - low[i][j] * low[m][j]
                pa[i] = pa[i] - low[i][j] * pa[j]
                pw[i] = pw[i] - low[i][j] * pw[j]
                if nx is not None:
                    nx[i] = nx[i] - low[i][j] * nx[j]
        rs.append(jnp.where(col >= row8 + base, stack(pa), 0.0))
        ws.append(stack(pw))
        if s + 1 < n:
            for m in range(8):
                a[s + 1] = a[s + 1] - nx[m] * pa[m]
                w[s + 1] = w[s + 1] - nx[m] * pw[m]
        if s + 2 < n:
            qa, qw = list(pa), list(pw)
            for m in reversed(range(8)):
                for i in range(m + 1, 8):
                    qa[m] = qa[m] - low[i][m] * qa[i]
                    qw[m] = qw[m] - low[i][m] * qw[i]
                qa[m] = qa[m] * inv[m]
                qw[m] = qw[m] * inv[m]
            for u in range(s + 2, n):
                for m in range(8):
                    c = lane(a[u], base + m)
                    if m == 0:
                        da, dw = c * qa[m], c * qw[m]
                    else:
                        da, dw = da + c * qa[m], dw + c * qw[m]
                a[u] = a[u] - da
                w[u] = w[u] - dw
    return rs, ws


def solve_kernel(x_ref, slope_ref, phi_ref, resid_ref, theta_ref, damp_ref,
                 r_ref, theta_out, pred_ref, a_ref, w_ref, g_ref):
    inv_total = 1.0 / x_ref[GRAD_ROW + 4:GRAD_ROW + 5, :]
    eye = (iota((NB, NB), 0) == iota((NB, NB), 1)).astype(F32) * damp_ref[0]
    for k, (i, j) in enumerate(BLOCKS):
        v = x_ref[k * NB:(k + 1) * NB, :] * inv_total
        if i == j:
            v = v + eye
        a_ref[i * NB:(i + 1) * NB, j * NB:(j + 1) * NB] = v
        if i != j:
            r_ref[j * NB:(j + 1) * NB, i * NB:(i + 1) * NB] = jnp.zeros((NB, NB), F32)
    for i in range(4):
        g_ref[i] = jnp.broadcast_to(x_ref[GRAD_ROW + i:GRAD_ROW + i + 1, :] * inv_total, (8, NB))

    def body(b, carry):
        at = pl.multiple_of(b * NB, NB)
        strips = [a_ref[pl.ds(at + 8 * s, 8), pl.ds(at, NB)] for s in range(16)]
        row8, col = iota((8, NB), 0), iota((8, NB), 1)
        ident = [(row8 + 8 * s == col).astype(F32) for s in range(16)]
        rs, ws = factor_block(strips, ident)
        for s in range(16):
            r_ref[pl.ds(at + 8 * s, 8), pl.ds(at, NB)] = rs[s]
            w_ref[b, 8 * s:8 * s + 8, :] = ws[s]
        g_ref[b] = dot(g_ref[b], w_ref[b], NT)
        for k in range(3):
            @pl.when(b == k)
            def _():
                lo, hi = k * NB, (k + 1) * NB
                panel = dot(w_ref[k], a_ref[lo:hi, hi:], NN)
                r_ref[lo:hi, hi:] = panel
                for c in range(k + 1, 4):
                    off = c * NB - hi
                    piece = panel[:, off:off + NB]
                    a_ref[c * NB:(c + 1) * NB, c * NB:] -= dot(piece, panel[:, off:], TN)
                    g_ref[c] = g_ref[c] - dot(g_ref[k], piece, NN)
        return carry

    lax.fori_loop(0, 4, body, 0)
    xs = [None] * 4
    for b in reversed(range(4)):
        z = g_ref[b]
        for c in range(b + 1, 4):
            z = z - dot(xs[c], r_ref[b * NB:(b + 1) * NB, c * NB:(c + 1) * NB], NT)
        xs[b] = dot(z, w_ref[b], NN)
    step_row = -jnp.concatenate(xs, axis=1)[0:1, :]
    chans, basis = theta_ref.shape
    own = (iota((chans, PARAMS), 1) >> 3) == iota((chans, PARAMS), 0)
    pick = ((iota((PARAMS, basis), 0) & 7) == iota((PARAMS, basis), 1)).astype(F32)
    step = dot(jnp.where(own, step_row, 0.0), pick, NN)
    theta_out[...] = theta_ref[...] + step
    moved = dot(step, phi_ref[...], NN)
    pred = resid_ref[...] + jnp.sum(slope_ref[...] * moved, axis=0, keepdims=True)
    pred_ref[...] = jnp.concatenate([pred[:, :NB], pred[:, NB:]], axis=0)


VM = pl.BlockSpec(memory_space=pltpu.VMEM)
SM = pl.BlockSpec(memory_space=pltpu.SMEM)


def sds(*shape):
    return jax.ShapeDtypeStruct(shape, F32)


def local_call(counts, img, pix, mask, targ, theta, amp):
    chans, basis = theta.shape
    slots = 256
    return pl.pallas_call(
        local_kernel,
        name="local",
        out_shape=(sds(ROWS, NB), sds(chans, slots), sds(basis, slots), sds(1, slots)),
        in_specs=[SM] + [VM] * 6,
        out_specs=(VM,) * 4,
    )(counts, img, pix, mask, targ, theta, amp)


def reduce_call(packed, ysize):
    dma = pltpu.SemaphoreType.DMA((16,))
    return pl.pallas_call(
        functools.partial(reduce_kernel, ysize),
        name="reduce",
        out_shape=sds(2, PLANE, CHUNK, NB),
        in_specs=[VM],
        out_specs=VM,
        scratch_shapes=[
            pltpu.VMEM((PLANE, CHUNK, NB), F32),
            pltpu.VMEM((PLANE, CHUNK, NB), F32),
            pltpu.VMEM((PLANE, CHUNK, NB), F32),
            pltpu.VMEM((ZN, ZROWS, NB), F32),
            pltpu.VMEM((ZN, ZROWS, NB), F32),
            pltpu.VMEM((ZN, ZROWS, NB), F32),
            pltpu.VMEM((2, PLANE, CHUNK, NB), F32),
        ] + [dma] * 12,
        compiler_params=pltpu.CompilerParams(collective_id=0, has_side_effects=True),
    )(packed.reshape(2, PLANE, CHUNK, NB))


def solve_call(summed, slope, phi, resid, theta, damping):
    slots = resid.shape[1]
    return pl.pallas_call(
        solve_kernel,
        name="solve",
        out_shape=(sds(PARAMS, PARAMS), sds(*theta.shape), sds(slots // NB, NB)),
        in_specs=[VM] * 5 + [SM],
        out_specs=(VM,) * 3,
        scratch_shapes=[
            pltpu.VMEM((PARAMS, PARAMS), F32),
            pltpu.VMEM((4, NB, NB), F32),
            pltpu.VMEM((4, 8, NB), F32),
        ],
    )(summed, slope, phi, resid, theta, damping)


def on_device(images, gauge_pixel, row_mask, gauge_counts, targets, theta, amplitude, damping):
    def lanes(v):
        return v.reshape(-1, NB)

    packed, slope, phi, resid = local_call(
        gauge_counts, images.reshape(-1, NB), lanes(gauge_pixel), lanes(row_mask),
        lanes(targets), theta, amplitude.reshape(-1, 1))
    summed = reduce_call(packed, 4)
    r, new_theta, pred = solve_call(
        summed.reshape(ROWS, NB), slope, phi, resid, theta, damping.reshape(1))
    return r, new_theta, pred.reshape(-1)


def solution(mesh):
    return jax.shard_map(
        on_device,
        mesh=mesh,
        in_specs=(P("rows", None, None), P("rows"), P("rows"), P("rows"), P("rows"), P(), P(), P()),
        out_specs=(P(), P(), P(("rows", "cols"))),
        check_vma=False,
    )
```

```python
import functools

import jax
import jax.numpy as jnp
import numpy as np
from jax import lax
from jax.experimental import pallas as pl
from jax.experimental.pallas import tpu as pltpu
from jax.sharding import PartitionSpec as P

HI = lax.Precision.HIGHEST
F32 = jnp.float32
NN = (((1,), (0,)), ((), ()))
NT = (((1,), (1,)), ((), ()))
TN = (((0,), (0,)), ((), ()))
MESH = pl.DeviceIdType.MESH

Y_KIND = [(0, 1.5), (1, 1.5), (0, 1.5), (2, 1.5), (1, 1.5), (0, 1.5), (0, 3.0), (0, 3.0)]
X_KIND = [(0, 1.5), (0, 1.5), (1, 1.5), (0, 1.5), (1, 1.5), (2, 1.5), (0, 3.0), (2, 3.0)]

NB = 128
PARAMS = 512
BLOCKS = [(i, j) for i in range(4) for j in range(i, 4)]
PLANE = 16
ZN = 16
ZROWS = 3
HALF = ZN // 2
PIECE = HALF * ZROWS
CHUNK = ZN * ZROWS
ROWS = 2 * PLANE * CHUNK
GRAD_ROW = len(BLOCKS) * NB


def dot(a, b, dims):
    return lax.dot_general(a, b, dims, precision=HI, preferred_element_type=F32)


def norm_of(order, width):
    t = np.arange(-12, 13).astype(np.float64)
    e = np.exp(-t * t / (2.0 * width * width))
    if order == 1:
        e = -t / width**2 * e
    if order == 2:
        e = (t * t / width**4 - 1.0 / width**2) * e
    return float(1.0 / np.sqrt(np.sum(e * e)))


def filters(t, kinds):
    t2 = t * t
    env = {w: jnp.exp(t2 * (-1.0 / (2.0 * w * w))) for w in sorted({w for _, w in kinds})}
    out = {}
    for order, w in sorted(set(kinds)):
        scale = norm_of(order, w)
        if order == 0:
            out[order, w] = env[w] * scale
        elif order == 1:
            out[order, w] = t * (-scale / w**2) * env[w]
        else:
            out[order, w] = (t2 * (scale / w**4) - scale / w**2) * env[w]
    return out


def iota(shape, dim):
    return lax.broadcasted_iota(jnp.int32, shape, dim)


def local_terms(count_ref, img_ref, pix_ref, mask_ref, targ_ref, theta_ref, amp_ref,
                slope_ref, phi_ref, resid_ref, packed_ref):
    col = lax.axis_index("cols")

    def own(ref):
        v = ref[pl.ds(2 * col, 2), :]
        return jnp.concatenate([v[0:1, :], v[1:2, :]], axis=1)

    pix = own(pix_ref)
    slots = pix.shape[1]
    place = col * slots + iota((1, slots), 1)
    live = ((place < count_ref[0]) & (own(mask_ref) == 1)).astype(F32)

    img = img_ref[...]
    src = iota((img.shape[0], slots), 0)
    row = pix >> 7
    near = (src >> 5) == (row >> 5)
    ty = ((row & 31) - (src & 31)).astype(F32)
    yk = filters(ty, Y_KIND)
    keys = sorted(yk)
    left = jnp.concatenate([jnp.where(near, yk[k], 0.0) for k in keys], axis=1)
    part = dot(img, left, TN)
    tx = ((pix & 127) - iota((img.shape[1], slots), 0)).astype(F32)
    xk = filters(tx, X_KIND)
    phis = []
    for ky, kx in zip(Y_KIND, X_KIND):
        at = keys.index(ky) * slots
        phis.append(jnp.sum(part[:, at:at + slots] * xk[kx], axis=0, keepdims=True))
    phi = jnp.concatenate(phis, axis=0)
    phi_ref[...] = phi

    act = jnp.tanh(dot(theta_ref[...], phi, TN))
    amp = jnp.transpose(jnp.broadcast_to(amp_ref[...], (NB, amp_ref.shape[1])))[:, 0:1]
    resid = live * (jnp.sum(amp * act, axis=0, keepdims=True) - own(targ_ref))
    resid_ref[...] = resid
    slope = live * amp * (1.0 - act * act)
    slope_ref[...] = slope
    jac = jnp.concatenate([slope[c:c + 1, :] * phi for c in range(slope.shape[0])], axis=0)

    for i in range(4):
        wide = dot(jac[i * NB:(i + 1) * NB], jac[i * NB:], NT)
        for j in range(i, 4):
            at = BLOCKS.index((i, j)) * NB
            packed_ref[at:at + NB, :] = wide[:, (j - i) * NB:(j - i + 1) * NB]
    grad = dot(jnp.broadcast_to(resid, (8, slots)), jac, NT)
    total = jnp.sum(live, axis=1, keepdims=True)
    rows = [grad[0:1, i * NB:(i + 1) * NB] for i in range(4)]
    rows += [jnp.broadcast_to(total, (1, NB)), jnp.zeros((3, NB), F32)]
    packed_ref[GRAD_ROW:GRAD_ROW + 8, :] = jnp.concatenate(rows, axis=0)
    packed_ref[GRAD_ROW + 8:, :] = jnp.zeros((ROWS - GRAD_ROW - 8, NB), F32)


def reduce_kernel(ysize, *refs):
    sum_ref, slope_ref, phi_ref, resid_ref = refs[7:11]
    own, got0, part, got1, zout, got2, zall, full = refs[11:19]
    (s0, r0), (s1, r1), (s2, r2), (s3, r3), (s4, r4), (s5, r5) = zip(refs[19::2], refs[20::2])
    row = lax.axis_index("rows")
    col = lax.axis_index("cols")
    y, z = row // ZN, lax.rem(row, ZN)
    x, core = col // 2, lax.rem(col, 2)
    me = x * ysize + y
    near = z // HALF
    far = 1 - near

    def at_plane(p):
        return {"rows": lax.rem(p, ysize) * ZN + z, "cols": (p // ysize) * 2 + core}

    def at_z(q):
        return {"rows": y * ZN + q, "cols": col}

    partner = {"rows": row, "cols": x * 2 + 1 - core}
    planes = [lax.rem(me + d, PLANE) for d in range(1, PLANE)]
    near_z = [near * HALF + lax.rem(z + d, HALF) for d in range(1, HALF)]
    far_z = [far * HALF + d for d in range(HALF)]

    barrier = pltpu.get_barrier_semaphore()
    for dev in [partner] + [at_plane(p) for p in planes] + [at_z(q) for q in near_z + far_z]:
        pl.semaphore_signal(barrier, inc=1, device_id=dev, device_id_type=MESH)

    local_terms(*refs[:7], slope_ref, phi_ref, resid_ref, own)

    pl.semaphore_wait(barrier, 1 + 2 * 15)

    sends = []

    def copy(src, dst, ssem, rsem, dev):
        return pltpu.make_async_remote_copy(
            src_ref=src, dst_ref=dst, send_sem=ssem, recv_sem=rsem,
            device_id=dev, device_id_type=MESH)

    def start(*args):
        c = copy(*args)
        c.start()
        sends.append(c)

    def rows_of(half_of, p, h):
        return pl.ds(pl.multiple_of((half_of * PLANE + p) * CHUNK + h * PIECE, 8), PIECE)

    order = planes + [me]
    for h in (far, near):
        for p in order:
            start(own.at[rows_of(1 - core, p, h)], got0.at[h, p], s0.at[h, p], r0.at[h, p], partner)
    for h in (far, near):
        for d, p in enumerate(order):
            mine = own.at[rows_of(core, p, h)]
            copy(mine, got0.at[h, p], s0.at[h, p], r0.at[h, p], partner).wait_recv()
            part[h, p] = mine[...] + got0[h, p]
            if d < PLANE - 1:
                start(part.at[h, p], got1.at[h, me], s1.at[h, p], r1.at[h, me], at_plane(p))
    for h, zs in ((far, far_z), (near, near_z)):
        acc = part[h, me]
        for p in planes:
            copy(part.at[h, p], got1.at[h, p], s1.at[h, p], r1.at[h, p], at_plane(p)).wait_recv()
            acc = acc + got1[h, p]
        for q in range(HALF):
            zout[h * HALF + q] = acc[q * ZROWS:(q + 1) * ZROWS, :]
        for q in zs:
            start(zout.at[q], got2.at[z], s2.at[q], r2.at[z], at_z(q))
    tot = zout[z]
    for q in near_z + far_z:
        copy(zout.at[q], got2.at[q], s2.at[q], r2.at[q], at_z(q)).wait_recv()
        tot = tot + got2[q]
    zall[z] = tot
    for q in far_z + near_z:
        start(zall.at[z], zall.at[z], s3.at[q], r3.at[z], at_z(q))
    for h, zs in ((near, near_z), (far, far_z)):
        for q in zs:
            copy(zall.at[q], zall.at[q], s3.at[q], r3.at[q], at_z(q)).wait_recv()
        block = full.at[rows_of(core, me, h)]
        block[...] = jnp.concatenate([zall[h * HALF + q] for q in range(HALF)], axis=0)
        for p in planes:
            start(block, block, s4.at[h, p], r4.at[h, me], at_plane(p))
        start(block, block, s5.at[h, me], r5.at[h, me], partner)
    for h in (near, far):
        for p in planes:
            block = full.at[rows_of(core, p, h)]
            copy(block, block, s4.at[h, p], r4.at[h, p], at_plane(p)).wait_recv()
            start(block, block, s5.at[h, p], r5.at[h, p], partner)
    for h in (near, far):
        for p in order:
            block = full.at[rows_of(1 - core, p, h)]
            copy(block, block, s5.at[h, p], r5.at[h, p], partner).wait_recv()
    for c in sends:
        c.wait_send()
    sum_ref[...] = full[...]


def lane(v, c):
    return jnp.take_along_axis(v, jnp.full((8, NB), c, jnp.int32), axis=1, mode="promise_in_bounds")


def sub(v, r):
    return jnp.broadcast_to(v[r:r + 1, :], (8, NB))


def factor_block(c):
    n = len(c)
    row8 = iota((8, NB), 0)
    col = iota((8, NB), 1)
    ws = []

    for s in range(n):
        base = 8 * s
        tile = (col >= base) & (col < base + 8)
        cb = [lane(c[s], base + m) for m in range(8)]
        t = [[sub(cb[m], i) if i >= m else None for m in range(8)] for i in range(8)]
        own = jnp.where(tile, (row8 + base == col).astype(F32), c[s])
        pa = [sub(own, i) for i in range(8)]
        nx = [lane(c[s + 1], base + m) for m in range(8)] if s + 1 < n else None
        rest = [[lane(c[u], base + m) for m in range(8)] for u in range(s + 2, n)]
        low = [[None] * 8 for _ in range(8)]
        inv = []
        for j in range(0, 8, 2):
            k = j + 1
            a11, a21, a22 = t[j][j], t[k][j], t[k][k]
            det = a11 * a22 - a21 * a21
            r1, r2 = lax.rsqrt(a11), lax.rsqrt(a11 * det)
            g1, g2 = a11 * r2, a21 * r2
            inv += [r1, g1]

            def pair(u, v):
                return u * r1, g1 * v - g2 * u

            low[k][j] = a21 * r1
            for i in range(j + 2, 8):
                low[i][j], low[i][k] = pair(t[i][j], t[i][k])
            for i in range(j + 2, 8):
                for m in range(j + 2, i + 1):
                    t[i][m] = t[i][m] - low[i][j] * low[m][j] - low[i][k] * low[m][k]
            rows = [pa] if nx is None else [pa, nx]
            for v in rows:
                v[j], v[k] = pair(v[j], v[k])
                for i in range(j + 2, 8):
                    v[i] = v[i] - low[i][j] * v[j] - low[i][k] * v[k]
        if s + 1 < n:
            d = [nx[m] * pa[m] for m in range(8)]
            d = ((d[0] + d[1]) + (d[2] + d[3])) + ((d[4] + d[5]) + (d[6] + d[7]))
            c[s + 1] = jnp.where(tile, 0.0, c[s + 1]) - d
        out = pa[0]
        for i in range(1, 8):
            out = jnp.where(row8 == i, pa[i], out)
        ws.append(jnp.where(col < base + 8, out, 0.0))
        if s + 2 < n:
            q = list(pa)
            for m in reversed(range(8)):
                for i in range(m + 1, 8):
                    q[m] = q[m] - low[i][m] * q[i]
                q[m] = q[m] * inv[m]
            for u in range(s + 2, n):
                cu = jnp.where(tile, 0.0, c[u])
                for m in range(8):
                    cu = cu - rest[u - s - 2][m] * q[m]
                c[u] = cu
    return ws


def solve_kernel(x_ref, slope_ref, phi_ref, resid_ref, theta_ref, damp_ref,
                 r_ref, theta_out, pred_ref, a_ref, w_ref, g_ref, y_ref):
    inv_total = 1.0 / x_ref[GRAD_ROW + 4:GRAD_ROW + 5, :]
    eye = (iota((NB, NB), 0) == iota((NB, NB), 1)).astype(F32) * damp_ref[0]
    upper = iota((NB, NB), 0) <= iota((NB, NB), 1)
    for k, (i, j) in enumerate(BLOCKS):
        v = x_ref[k * NB:(k + 1) * NB, :] * inv_total
        if i == j:
            v = v + eye
        else:
            r_ref[j * NB:(j + 1) * NB, i * NB:(i + 1) * NB] = jnp.zeros((NB, NB), F32)
        a_ref[i * NB:(i + 1) * NB, j * NB:(j + 1) * NB] = v
    for i in range(4):
        g_ref[i] = x_ref[GRAD_ROW + i:GRAD_ROW + i + 1, :] * inv_total

    def body(b, carry):
        at = pl.multiple_of(b * NB, NB)
        ws = factor_block([a_ref[pl.ds(at + 8 * s, 8), pl.ds(at, NB)] for s in range(16)])
        for s in range(16):
            w_ref[b, 8 * s:8 * s + 8, :] = ws[s]
        for k in range(4):
            @pl.when(b == k)
            def _():
                lo, hi = k * NB, (k + 1) * NB
                w = w_ref[k]
                panel = dot(w, a_ref[lo:hi, lo:], NN)
                r_ref[lo:hi, lo:hi] = jnp.where(upper, panel[:, :NB], 0.0)
                y = jnp.sum(w * g_ref[k], axis=1, keepdims=True)
                y_ref[k] = y
                if k < 3:
                    r_ref[lo:hi, hi:] = panel[:, NB:]
                for c in range(k + 1, 4):
                    off = c * NB - lo
                    piece = panel[:, off:off + NB]
                    a_ref[c * NB:(c + 1) * NB, c * NB:] -= dot(piece, panel[:, off:], TN)
                    g_ref[c] = g_ref[c] - jnp.sum(piece * y, axis=0, keepdims=True)
        return carry

    lax.fori_loop(0, 4, body, 0)
    xs = [None] * 4
    for b in reversed(range(4)):
        z = y_ref[b]
        if b < 3:
            d = r_ref[b * NB:(b + 1) * NB, (b + 1) * NB:(b + 2) * NB] * xs[b + 1]
            for c in range(b + 2, 4):
                d = d + r_ref[b * NB:(b + 1) * NB, c * NB:(c + 1) * NB] * xs[c]
            z = z - jnp.sum(d, axis=1, keepdims=True)
        xs[b] = jnp.sum(w_ref[b] * z, axis=0, keepdims=True)
    step_row = -jnp.concatenate(xs, axis=1)
    basis, chans = theta_ref.shape
    own = (iota((basis, PARAMS), 1) & 7) == iota((basis, PARAMS), 0)
    pick = ((iota((PARAMS, chans), 0) >> 3) == iota((PARAMS, chans), 1)).astype(F32)
    step = dot(jnp.where(own, step_row, 0.0), pick, NN)
    theta_out[...] = theta_ref[...] + step
    moved = dot(step, phi_ref[...], TN)
    pred = resid_ref[...] + jnp.sum(slope_ref[...] * moved, axis=0, keepdims=True)
    pred_ref[...] = jnp.concatenate([pred[:, :NB], pred[:, NB:]], axis=0)


THETA_T = True
VM = pl.BlockSpec(memory_space=pltpu.VMEM)
SM = pl.BlockSpec(memory_space=pltpu.SMEM)


def sds(*shape):
    return jax.ShapeDtypeStruct(shape, F32)


def reduce_call(ysize, *args):
    basis, chans = args[5].shape
    slots = 256
    pair, line = pltpu.SemaphoreType.DMA((2, PLANE)), pltpu.SemaphoreType.DMA((ZN,))
    return pl.pallas_call(
        functools.partial(reduce_kernel, ysize),
        name="reduce",
        out_shape=(sds(ROWS, NB), sds(chans, slots), sds(basis, slots), sds(1, slots)),
        in_specs=[SM] + [VM] * 6,
        out_specs=(VM,) * 4,
        scratch_shapes=[
            pltpu.VMEM((ROWS, NB), F32),
            pltpu.VMEM((2, PLANE, PIECE, NB), F32),
            pltpu.VMEM((2, PLANE, PIECE, NB), F32),
            pltpu.VMEM((2, PLANE, PIECE, NB), F32),
            pltpu.VMEM((ZN, ZROWS, NB), F32),
            pltpu.VMEM((ZN, ZROWS, NB), F32),
            pltpu.VMEM((ZN, ZROWS, NB), F32),
            pltpu.VMEM((ROWS, NB), F32),
        ] + [pair] * 4 + [line] * 4 + [pair] * 4,
        compiler_params=pltpu.CompilerParams(collective_id=0, has_side_effects=True),
    )(*args)


def solve_call(summed, slope, phi, resid, theta, damping):
    slots = resid.shape[1]
    return pl.pallas_call(
        solve_kernel,
        name="solve",
        out_shape=(sds(PARAMS, PARAMS), sds(*theta.shape), sds(slots // NB, NB)),
        in_specs=[VM] * 5 + [SM],
        out_specs=(VM,) * 3,
        scratch_shapes=[
            pltpu.VMEM((PARAMS, PARAMS), F32),
            pltpu.VMEM((4, NB, NB), F32),
            pltpu.VMEM((4, 1, NB), F32),
            pltpu.VMEM((4, NB, 1), F32),
        ],
    )(summed, slope, phi, resid, theta, damping)


def on_device(images, gauge_pixel, row_mask, gauge_counts, targets, theta, amplitude, damping):
    def lanes(v):
        return v.reshape(-1, NB)

    summed, slope, phi, resid = reduce_call(
        4, gauge_counts, images.reshape(-1, NB), lanes(gauge_pixel), lanes(row_mask),
        lanes(targets), theta.T, amplitude.reshape(1, -1))
    r, new_theta, pred = solve_call(
        summed, slope, phi, resid, theta.T, damping.reshape(1))
    return r, new_theta.T, pred.reshape(-1)


def solution(mesh):
    return jax.shard_map(
        on_device,
        mesh=mesh,
        in_specs=(P("rows", None, None), P("rows"), P("rows"), P("rows"), P("rows"), P(), P(), P()),
        out_specs=(P(), P(), P(("rows", "cols"))),
        check_vma=False,
    )
```

```python
import functools

import jax
import jax.numpy as jnp
import numpy as np
from jax import lax
from jax.experimental import pallas as pl
from jax.experimental.pallas import tpu as pltpu
from jax.sharding import PartitionSpec as P

HI = lax.Precision.HIGHEST
F32 = jnp.float32
NN = (((1,), (0,)), ((), ()))
NT = (((1,), (1,)), ((), ()))
TN = (((0,), (0,)), ((), ()))
MESH = pl.DeviceIdType.MESH

Y_KIND = [(0, 1.5), (1, 1.5), (0, 1.5), (2, 1.5), (1, 1.5), (0, 1.5), (0, 3.0), (0, 3.0)]
X_KIND = [(0, 1.5), (0, 1.5), (1, 1.5), (0, 1.5), (1, 1.5), (2, 1.5), (0, 3.0), (2, 3.0)]

NB = 128
PARAMS = 512
BLOCKS = [(0, 0), (0, 1), (0, 2), (0, 3), (1, 2), (1, 3), (2, 2), (2, 3)]
PLANE = 16
ZN = 16
QUARTERS = 4
ROWS = len(BLOCKS) * NB
EXTRA = 8


def dot(a, b, dims):
    return lax.dot_general(a, b, dims, precision=HI, preferred_element_type=F32)


def norm_of(order, width):
    t = np.arange(-12, 13).astype(np.float64)
    e = np.exp(-t * t / (2.0 * width * width))
    if order == 1:
        e = -t / width**2 * e
    if order == 2:
        e = (t * t / width**4 - 1.0 / width**2) * e
    return float(1.0 / np.sqrt(np.sum(e * e)))


def filters(t, kinds):
    t2 = t * t
    env = {w: jnp.exp(t2 * (-1.0 / (2.0 * w * w))) for w in sorted({w for _, w in kinds})}
    out = {}
    for order, w in sorted(set(kinds)):
        scale = norm_of(order, w)
        if order == 0:
            out[order, w] = env[w] * scale
        elif order == 1:
            out[order, w] = t * (-scale / w**2) * env[w]
        else:
            out[order, w] = (t2 * (scale / w**4) - scale / w**2) * env[w]
    return out


def iota(shape, dim):
    return lax.broadcasted_iota(jnp.int32, shape, dim)


def local_terms(count_ref, img_ref, pix_ref, mask_ref, targ_ref, theta_ref, amp_ref,
                slope_ref, phi_ref, resid_ref, packed_ref):
    col = lax.axis_index("cols")

    def own(ref):
        v = ref[pl.ds(2 * col, 2), :]
        return jnp.concatenate([v[0:1, :], v[1:2, :]], axis=1)

    pix = own(pix_ref)
    slots = pix.shape[1]
    place = col * slots + iota((1, slots), 1)
    live = ((place < count_ref[0]) & (own(mask_ref) == 1)).astype(F32)

    img = img_ref[...]
    src = iota((img.shape[0], slots), 0)
    row = pix >> 7
    near = (src >> 5) == (row >> 5)
    ty = ((row & 31) - (src & 31)).astype(F32)
    yk = filters(ty, Y_KIND)
    keys = sorted(yk)
    left = jnp.concatenate([jnp.where(near, yk[k], 0.0) for k in keys], axis=1)
    part = dot(img, left, TN)
    tx = ((pix & 127) - iota((img.shape[1], slots), 0)).astype(F32)
    xk = filters(tx, X_KIND)
    phis = []
    for ky, kx in zip(Y_KIND, X_KIND):
        at = keys.index(ky) * slots
        phis.append(jnp.sum(part[:, at:at + slots] * xk[kx], axis=0, keepdims=True))
    phi = jnp.concatenate(phis, axis=0)
    phi_ref[...] = phi

    act = jnp.tanh(dot(theta_ref[...], phi, TN))
    amp = jnp.transpose(jnp.broadcast_to(amp_ref[...], (NB, amp_ref.shape[1])))[:, 0:1]
    resid = live * (jnp.sum(amp * act, axis=0, keepdims=True) - own(targ_ref))
    resid_ref[...] = resid
    slope = live * amp * (1.0 - act * act)
    slope_ref[...] = slope
    jac = jnp.concatenate([slope[c:c + 1, :] * phi for c in range(slope.shape[0])], axis=0)

    upper = iota((NB, NB), 0) <= iota((NB, NB), 1)
    diag = iota((NB, NB), 0) == iota((NB, NB), 1)
    rows = []
    for i in range(4):
        wide = dot(jac[i * NB:(i + 1) * NB], jac[i * NB:], NT)
        for j in range(i, 4):
            block = wide[:, (j - i) * NB:(j - i + 1) * NB]
            if i == j and i % 2 == 0:
                first = block
                continue
            at = BLOCKS.index((i - 1, i - 1) if i == j else (i, j)) * NB
            if i == j:
                rows.append(jnp.sum(jnp.where(diag, block, 0.0), axis=0, keepdims=True))
                block = jnp.where(upper, first, block)
            packed_ref[at:at + NB, :] = block
    grad = dot(jnp.broadcast_to(resid, (8, slots)), jac, NT)
    total = jnp.sum(live, axis=1, keepdims=True)
    rows = [grad[0:1, i * NB:(i + 1) * NB] for i in range(4)] + rows
    rows += [jnp.broadcast_to(total, (1, NB)), jnp.zeros((1, NB), F32)]
    return jnp.concatenate(rows, axis=0)


def reduce_kernel(ysize, *refs):
    sum_ref, slope_ref, phi_ref, resid_ref = refs[7:11]
    own, got0, part, got1, zout, got2, zall, full, e0, e1, e2 = refs[11:22]
    (s0, r0), (s1, r1), (s2, r2), (s3, r3), (s4, r4), (s5, r5) = zip(refs[22:34:2], refs[23:34:2])
    (t0, v0), (t1, v1), (t2, v2) = zip(refs[34::2], refs[35::2])
    row = lax.axis_index("rows")
    col = lax.axis_index("cols")
    y, z = row // ZN, lax.rem(row, ZN)
    x, core = col // 2, lax.rem(col, 2)
    me = x * ysize + y
    near = z // QUARTERS
    far_first = [lax.rem(near + d, QUARTERS) for d in (2, 1, 3, 0)]

    def at_plane(p):
        return {"rows": lax.rem(p, ysize) * ZN + z, "cols": (p // ysize) * 2 + core}

    def at_z(q):
        return {"rows": y * ZN + q, "cols": col}

    partner = {"rows": row, "cols": x * 2 + 1 - core}
    planes = [lax.rem(me + d, PLANE) for d in range(1, PLANE)]
    peers = [[k * 4 + d for d in range(4)] for k in far_first[:3]]
    peers.append([near * 4 + lax.rem(z + d, 4) for d in range(1, 4)])
    zs = [q for group in peers for q in group]

    barrier = pltpu.get_barrier_semaphore()
    for dev in [partner] + [at_plane(p) for p in planes] + [at_z(q) for q in zs]:
        pl.semaphore_signal(barrier, inc=1, device_id=dev, device_id_type=MESH)

    e0[core] = local_terms(*refs[:7], slope_ref, phi_ref, resid_ref, own)

    pl.semaphore_wait(barrier, 1 + 2 * 15)

    sends = []

    def copy(src, dst, ssem, rsem, dev):
        return pltpu.make_async_remote_copy(
            src_ref=src, dst_ref=dst, send_sem=ssem, recv_sem=rsem,
            device_id=dev, device_id_type=MESH)

    def start(*args):
        c = copy(*args)
        c.start()
        sends.append(c)

    def block(half, k):
        return pl.ds(pl.multiple_of((half * QUARTERS + k) * NB, NB), NB)

    def tile(p):
        return pl.ds(pl.multiple_of(p * 8, 8), 8)

    def tile_of(half, k, p):
        return pl.ds(pl.multiple_of((half * QUARTERS + k) * NB + p * 8, 8), 8)

    for k in far_first:
        start(own.at[block(1 - core, k)], got0.at[k], s0.at[k], r0.at[k], partner)
    start(e0.at[core], e0.at[core], t0, v0, partner)
    for k in far_first:
        mine = own.at[block(core, k)]
        copy(mine, got0.at[k], s0.at[k], r0.at[k], partner).wait_recv()
        part[k] = mine[...] + got0[k]
        for p in planes:
            start(part.at[k, tile(p)], got1.at[k, me], s1.at[k, p], r1.at[k, me], at_plane(p))
    copy(e0.at[1 - core], e0.at[1 - core], t0, v0, partner).wait_recv()
    e1[me] = e0[0] + e0[1]
    for p in planes:
        start(e1.at[me], e1.at[me], t1.at[p], v1.at[me], at_plane(p))
    for k, group in zip(far_first, peers):
        acc = part[k, tile(me)]
        for p in planes:
            copy(part.at[k, tile(p)], got1.at[k, p], s1.at[k, p], r1.at[k, p], at_plane(p)).wait_recv()
            acc = acc + got1[k, p]
        for d in range(4):
            zout[k * 4 + d] = acc[2 * d:2 * d + 2, :]
        for q in group:
            start(zout.at[q], got2.at[z], s2.at[q], r2.at[z], at_z(q))
    for p in planes:
        copy(e1.at[p], e1.at[p], t1.at[p], v1.at[p], at_plane(p)).wait_recv()
    acc = e1[0]
    for p in range(1, PLANE):
        acc = acc + e1[p]
    e2[z] = acc
    for q in zs:
        start(e2.at[z], e2.at[z], t2.at[q], v2.at[z], at_z(q))
    tot = zout[z]
    for q in reversed(zs):
        copy(zout.at[q], got2.at[q], s2.at[q], r2.at[q], at_z(q)).wait_recv()
        tot = tot + got2[q]
    zall[z] = tot
    for q in zs:
        start(zall.at[z], zall.at[z], s3.at[q], r3.at[z], at_z(q))
    near_first = list(reversed(far_first))
    for k, group in zip(near_first, reversed(peers)):
        for q in group:
            copy(zall.at[q], zall.at[q], s3.at[q], r3.at[q], at_z(q)).wait_recv()
        mine = full.at[tile_of(core, k, me)]
        mine[...] = jnp.concatenate([zall[k * 4 + d] for d in range(4)], axis=0)
        for p in planes:
            start(mine, mine, s4.at[k, p], r4.at[k, me], at_plane(p))
    for q in zs:
        copy(e2.at[q], e2.at[q], t2.at[q], v2.at[q], at_z(q)).wait_recv()
    acc = e2[0]
    for q in range(1, ZN):
        acc = acc + e2[q]
    sum_ref[ROWS:ROWS + EXTRA, :] = acc
    for k in near_first:
        for p in planes:
            got = full.at[tile_of(core, k, p)]
            copy(got, got, s4.at[k, p], r4.at[k, p], at_plane(p)).wait_recv()
        mine = full.at[block(core, k)]
        start(mine, mine, s5.at[k], r5.at[k], partner)
    for k in near_first:
        got = full.at[block(1 - core, k)]
        copy(got, got, s5.at[k], r5.at[k], partner).wait_recv()
    for c in sends:
        c.wait_send()
    sum_ref[0:ROWS, :] = full[...]


def lane(v, c):
    return jnp.take_along_axis(v, jnp.full((8, NB), c, jnp.int32), axis=1, mode="promise_in_bounds")


def sub(v, r):
    return jnp.broadcast_to(v[r:r + 1, :], (8, NB))


def factor_block(c):
    n = len(c)
    row8 = iota((8, NB), 0)
    col = iota((8, NB), 1)
    ws = []

    for s in range(n):
        base = 8 * s
        tile = (col >= base) & (col < base + 8)
        cb = [lane(c[s], base + m) for m in range(8)]
        t = [[sub(cb[m], i) if i >= m else None for m in range(8)] for i in range(8)]
        own = jnp.where(tile, (row8 + base == col).astype(F32), c[s])
        pa = [sub(own, i) for i in range(8)]
        nx = [lane(c[s + 1], base + m) for m in range(8)] if s + 1 < n else None
        rest = [[lane(c[u], base + m) for m in range(8)] for u in range(s + 2, n)]
        low = [[None] * 8 for _ in range(8)]
        inv = []
        for j in range(0, 8, 2):
            k = j + 1
            a11, a21, a22 = t[j][j], t[k][j], t[k][k]
            det = a11 * a22 - a21 * a21
            r1, r2 = lax.rsqrt(a11), lax.rsqrt(a11 * det)
            g1, g2 = a11 * r2, a21 * r2
            inv += [r1, g1]

            def pair(u, v):
                return u * r1, g1 * v - g2 * u

            low[k][j] = a21 * r1
            for i in range(j + 2, 8):
                low[i][j], low[i][k] = pair(t[i][j], t[i][k])
            for i in range(j + 2, 8):
                for m in range(j + 2, i + 1):
                    t[i][m] = t[i][m] - low[i][j] * low[m][j] - low[i][k] * low[m][k]
            rows = [pa] if nx is None else [pa, nx]
            for v in rows:
                v[j], v[k] = pair(v[j], v[k])
                for i in range(j + 2, 8):
                    v[i] = v[i] - low[i][j] * v[j] - low[i][k] * v[k]
        if s + 1 < n:
            d = [nx[m] * pa[m] for m in range(8)]
            d = ((d[0] + d[1]) + (d[2] + d[3])) + ((d[4] + d[5]) + (d[6] + d[7]))
            c[s + 1] = jnp.where(tile, 0.0, c[s + 1]) - d
        out = pa[0]
        for i in range(1, 8):
            out = jnp.where(row8 == i, pa[i], out)
        ws.append(jnp.where(col < base + 8, out, 0.0))
        if s + 2 < n:
            q = list(pa)
            for m in reversed(range(8)):
                for i in range(m + 1, 8):
                    q[m] = q[m] - low[i][m] * q[i]
                q[m] = q[m] * inv[m]
            for u in range(s + 2, n):
                cu = jnp.where(tile, 0.0, c[u])
                for m in range(8):
                    cu = cu - rest[u - s - 2][m] * q[m]
                c[u] = cu
    return ws


def solve_kernel(x_ref, slope_ref, phi_ref, resid_ref, theta_ref, damp_ref,
                 r_ref, theta_out, pred_ref, a_ref, w_ref, g_ref, y_ref):
    inv_total = 1.0 / x_ref[ROWS + 6:ROWS + 7, :]
    same = iota((NB, NB), 0) == iota((NB, NB), 1)
    eye = same.astype(F32) * damp_ref[0]
    upper = iota((NB, NB), 0) <= iota((NB, NB), 1)
    for k, (i, j) in enumerate(BLOCKS):
        v = x_ref[k * NB:(k + 1) * NB, :] * inv_total
        if i == j:
            t = jnp.transpose(v)
            low = jnp.where(upper, t, v)
            row = ROWS + 4 + i // 2
            low = jnp.where(same, x_ref[row:row + 1, :] * inv_total, low)
            a_ref[i * NB:(i + 1) * NB, i * NB:(i + 1) * NB] = jnp.where(upper, v, t) + eye
            i, v = i + 1, low + eye
            a_ref[i * NB:(i + 1) * NB, i * NB:(i + 1) * NB] = v
        else:
            a_ref[i * NB:(i + 1) * NB, j * NB:(j + 1) * NB] = v
    for i in range(4):
        for j in range(i):
            r_ref[i * NB:(i + 1) * NB, j * NB:(j + 1) * NB] = jnp.zeros((NB, NB), F32)
        g_ref[i] = x_ref[ROWS + i:ROWS + i + 1, :] * inv_total

    def body(b, carry):
        at = pl.multiple_of(b * NB, NB)
        ws = factor_block([a_ref[pl.ds(at + 8 * s, 8), pl.ds(at, NB)] for s in range(16)])
        for s in range(16):
            w_ref[b, 8 * s:8 * s + 8, :] = ws[s]
        for k in range(4):
            @pl.when(b == k)
            def _():
                lo, hi = k * NB, (k + 1) * NB
                w = w_ref[k]
                panel = dot(w, a_ref[lo:hi, lo:], NN)
                r_ref[lo:hi, lo:hi] = jnp.where(upper, panel[:, :NB], 0.0)
                y = jnp.sum(w * g_ref[k], axis=1, keepdims=True)
                y_ref[k] = y
                if k < 3:
                    r_ref[lo:hi, hi:] = panel[:, NB:]
                for c in range(k + 1, 4):
                    off = c * NB - lo
                    piece = panel[:, off:off + NB]
                    a_ref[c * NB:(c + 1) * NB, c * NB:] -= dot(piece, panel[:, off:], TN)
                    g_ref[c] = g_ref[c] - jnp.sum(piece * y, axis=0, keepdims=True)
        return carry

    lax.fori_loop(0, 4, body, 0)
    xs = [None] * 4
    for b in reversed(range(4)):
        z = y_ref[b]
        if b < 3:
            d = r_ref[b * NB:(b + 1) * NB, (b + 1) * NB:(b + 2) * NB] * xs[b + 1]
            for c in range(b + 2, 4):
                d = d + r_ref[b * NB:(b + 1) * NB, c * NB:(c + 1) * NB] * xs[c]
            z = z - jnp.sum(d, axis=1, keepdims=True)
        xs[b] = jnp.sum(w_ref[b] * z, axis=0, keepdims=True)
    step_row = -jnp.concatenate(xs, axis=1)
    basis, chans = theta_ref.shape
    own = (iota((basis, PARAMS), 1) & 7) == iota((basis, PARAMS), 0)
    pick = ((iota((PARAMS, chans), 0) >> 3) == iota((PARAMS, chans), 1)).astype(F32)
    step = dot(jnp.where(own, step_row, 0.0), pick, NN)
    theta_out[...] = theta_ref[...] + step
    moved = dot(step, phi_ref[...], TN)
    pred = resid_ref[...] + jnp.sum(slope_ref[...] * moved, axis=0, keepdims=True)
    pred_ref[...] = jnp.concatenate([pred[:, :NB], pred[:, NB:]], axis=0)


THETA_T = True
VM = pl.BlockSpec(memory_space=pltpu.VMEM)
SM = pl.BlockSpec(memory_space=pltpu.SMEM)


def sds(*shape):
    return jax.ShapeDtypeStruct(shape, F32)


def reduce_call(ysize, *args):
    basis, chans = args[5].shape
    slots = 256
    dma = pltpu.SemaphoreType.DMA
    four, grid, line = dma((QUARTERS,)), dma((QUARTERS, PLANE)), dma((ZN,))
    return pl.pallas_call(
        functools.partial(reduce_kernel, ysize),
        name="reduce",
        out_shape=(sds(ROWS + EXTRA, NB), sds(chans, slots), sds(basis, slots), sds(1, slots)),
        in_specs=[SM] + [VM] * 6,
        out_specs=(VM,) * 4,
        scratch_shapes=[
            pltpu.VMEM((ROWS, NB), F32),
            pltpu.VMEM((QUARTERS, NB, NB), F32),
            pltpu.VMEM((QUARTERS, NB, NB), F32),
            pltpu.VMEM((QUARTERS, PLANE, 8, NB), F32),
            pltpu.VMEM((ZN, 2, NB), F32),
            pltpu.VMEM((ZN, 2, NB), F32),
            pltpu.VMEM((ZN, 2, NB), F32),
            pltpu.VMEM((ROWS, NB), F32),
            pltpu.VMEM((2, 8, NB), F32),
            pltpu.VMEM((PLANE, 8, NB), F32),
            pltpu.VMEM((ZN, 8, NB), F32),
        ] + [four] * 2 + [grid] * 2 + [line] * 4 + [grid] * 2 + [four] * 2 + [dma] * 2 + [line] * 4,
        compiler_params=pltpu.CompilerParams(collective_id=0, has_side_effects=True),
    )(*args)


def solve_call(summed, slope, phi, resid, theta, damping):
    slots = resid.shape[1]
    return pl.pallas_call(
        solve_kernel,
        name="solve",
        out_shape=(sds(PARAMS, PARAMS), sds(*theta.shape), sds(slots // NB, NB)),
        in_specs=[VM] * 5 + [SM],
        out_specs=(VM,) * 3,
        scratch_shapes=[
            pltpu.VMEM((PARAMS, PARAMS), F32),
            pltpu.VMEM((4, NB, NB), F32),
            pltpu.VMEM((4, 1, NB), F32),
            pltpu.VMEM((4, NB, 1), F32),
        ],
    )(summed, slope, phi, resid, theta, damping)


def on_device(images, gauge_pixel, row_mask, gauge_counts, targets, theta, amplitude, damping):
    def lanes(v):
        return v.reshape(-1, NB)

    summed, slope, phi, resid = reduce_call(
        4, gauge_counts, images.reshape(-1, NB), lanes(gauge_pixel), lanes(row_mask),
        lanes(targets), theta.T, amplitude.reshape(1, -1))
    r, new_theta, pred = solve_call(
        summed, slope, phi, resid, theta.T, damping.reshape(1))
    return r, new_theta.T, pred.reshape(-1)


def solution(mesh):
    return jax.shard_map(
        on_device,
        mesh=mesh,
        in_specs=(P("rows", None, None), P("rows"), P("rows"), P("rows"), P("rows"), P(), P(), P()),
        out_specs=(P(), P(), P(("rows", "cols"))),
        check_vma=False,
    )
```

```python
import functools

import jax
import jax.numpy as jnp
import numpy as np
from jax import lax
from jax.experimental import pallas as pl
from jax.experimental.pallas import tpu as pltpu
from jax.sharding import PartitionSpec as P

HI = lax.Precision.HIGHEST
F32 = jnp.float32
NN = (((1,), (0,)), ((), ()))
NT = (((1,), (1,)), ((), ()))
TN = (((0,), (0,)), ((), ()))
MESH = pl.DeviceIdType.MESH

Y_KIND = [(0, 1.5), (1, 1.5), (0, 1.5), (2, 1.5), (1, 1.5), (0, 1.5), (0, 3.0), (0, 3.0)]
X_KIND = [(0, 1.5), (0, 1.5), (1, 1.5), (0, 1.5), (1, 1.5), (2, 1.5), (0, 3.0), (2, 3.0)]

NB = 128
PARAMS = 512
BLOCKS = [(0, 0), (0, 1), (0, 2), (0, 3), (1, 2), (1, 3), (2, 2), (2, 3)]
PLANE = 16
ZN = 16
QUARTERS = 4
ROWS = len(BLOCKS) * NB
EXTRA = 8
DAMP_ROW = ROWS + EXTRA - 1


def dot(a, b, dims):
    return lax.dot_general(a, b, dims, precision=HI, preferred_element_type=F32)


def norm_of(order, width):
    t = np.arange(-12, 13).astype(np.float64)
    e = np.exp(-t * t / (2.0 * width * width))
    if order == 1:
        e = -t / width**2 * e
    if order == 2:
        e = (t * t / width**4 - 1.0 / width**2) * e
    return float(1.0 / np.sqrt(np.sum(e * e)))


def filters(t, kinds):
    t2 = t * t
    env = {w: jnp.exp(t2 * (-1.0 / (2.0 * w * w))) for w in sorted({w for _, w in kinds})}
    out = {}
    for order, w in sorted(set(kinds)):
        scale = norm_of(order, w)
        if order == 0:
            out[order, w] = env[w] * scale
        elif order == 1:
            out[order, w] = t * (-scale / w**2) * env[w]
        else:
            out[order, w] = (t2 * (scale / w**4) - scale / w**2) * env[w]
    return out


def iota(shape, dim):
    return lax.broadcasted_iota(jnp.int32, shape, dim)


def local_terms(count_ref, img_ref, pix_ref, mask_ref, targ_ref, theta_ref, amp_ref,
                slope_ref, phi_ref, resid_ref, packed_ref):
    col = lax.axis_index("cols")

    def own(ref):
        v = ref[pl.ds(2 * col, 2), :]
        return jnp.concatenate([v[0:1, :], v[1:2, :]], axis=1)

    pix = own(pix_ref)
    slots = pix.shape[1]
    place = col * slots + iota((1, slots), 1)
    live = ((place < count_ref[...]) & (own(mask_ref) == 1)).astype(F32)

    img = img_ref[...]
    src = iota((img.shape[0], slots), 0)
    row = pix >> 7
    near = (src >> 5) == (row >> 5)
    ty = ((row & 31) - (src & 31)).astype(F32)
    yk = filters(ty, Y_KIND)
    keys = sorted(yk)
    left = jnp.concatenate([jnp.where(near, yk[k], 0.0) for k in keys], axis=1)
    part = dot(img, left, TN)
    tx = ((pix & 127) - iota((img.shape[1], slots), 0)).astype(F32)
    xk = filters(tx, X_KIND)
    phis = []
    for ky, kx in zip(Y_KIND, X_KIND):
        at = keys.index(ky) * slots
        phis.append(jnp.sum(part[:, at:at + slots] * xk[kx], axis=0, keepdims=True))
    phi = jnp.concatenate(phis, axis=0)
    phi_ref[...] = phi

    act = jnp.tanh(dot(theta_ref[...], phi, TN))
    amp = jnp.transpose(jnp.broadcast_to(amp_ref[...], (NB, amp_ref.shape[1])))[:, 0:1]
    resid = live * (jnp.sum(amp * act, axis=0, keepdims=True) - own(targ_ref))
    resid_ref[...] = resid
    slope = live * amp * (1.0 - act * act)
    slope_ref[...] = slope
    jac = jnp.concatenate([slope[c:c + 1, :] * phi for c in range(slope.shape[0])], axis=0)

    upper = iota((NB, NB), 0) <= iota((NB, NB), 1)
    diag = iota((NB, NB), 0) == iota((NB, NB), 1)
    rows = []
    for i in range(4):
        wide = dot(jac[i * NB:(i + 1) * NB], jac[i * NB:], NT)
        for j in range(i, 4):
            block = wide[:, (j - i) * NB:(j - i + 1) * NB]
            if i == j and i % 2 == 0:
                first = block
                continue
            at = BLOCKS.index((i - 1, i - 1) if i == j else (i, j)) * NB
            if i == j:
                rows.append(jnp.sum(jnp.where(diag, block, 0.0), axis=0, keepdims=True))
                block = jnp.where(upper, first, block)
            packed_ref[at:at + NB, :] = block
    grad = dot(jnp.broadcast_to(resid, (8, slots)), jac, NT)
    total = jnp.sum(live, axis=1, keepdims=True)
    rows = [grad[0:1, i * NB:(i + 1) * NB] for i in range(4)] + rows
    rows += [jnp.broadcast_to(total, (1, NB)), jnp.zeros((1, NB), F32)]
    return jnp.concatenate(rows, axis=0)


def reduce_kernel(ysize, *refs):
    args, held, in_sems = refs[:8], refs[13:21], refs[21]
    sum_ref, slope_ref, phi_ref, resid_ref, theta_out = refs[8:13]
    refs = refs[22:]
    own, got0, part, got1, zout, got2, zall, full, e0, e1, e2 = refs[:11]
    (s0, r0), (s1, r1), (s2, r2), (s3, r3), (s4, r4), (s5, r5) = zip(refs[11:23:2], refs[12:23:2])
    (t0, v0), (t1, v1), (t2, v2) = zip(refs[23::2], refs[24::2])
    row = lax.axis_index("rows")
    col = lax.axis_index("cols")
    y, z = row // ZN, lax.rem(row, ZN)
    x, core = col // 2, lax.rem(col, 2)
    me = x * ysize + y
    near = z // QUARTERS
    far_first = [lax.rem(near + d, QUARTERS) for d in (2, 1, 3, 0)]

    def at_plane(p):
        return {"rows": lax.rem(p, ysize) * ZN + z, "cols": (p // ysize) * 2 + core}

    def at_z(q):
        return {"rows": y * ZN + q, "cols": col}

    partner = {"rows": row, "cols": x * 2 + 1 - core}
    planes = [lax.rem(me + d, PLANE) for d in range(1, PLANE)]
    peers = [[k * 4 + d for d in range(4)] for k in far_first[:3]]
    peers.append([near * 4 + lax.rem(z + d, 4) for d in range(1, 4)])
    zs = [q for group in peers for q in group]

    loads = [pltpu.make_async_copy(a, h, in_sems.at[i]) for i, (a, h) in enumerate(zip(args, held))]
    for c in loads:
        c.start()

    barrier = pltpu.get_barrier_semaphore()
    for dev in [partner] + [at_plane(p) for p in planes] + [at_z(q) for q in zs]:
        pl.semaphore_signal(barrier, inc=1, device_id=dev, device_id_type=MESH)

    for c in loads:
        c.wait()
    theta_out[...] = held[5][...]
    e0[core] = local_terms(*held[:7], slope_ref, phi_ref, resid_ref, own)

    pl.semaphore_wait(barrier, 1 + 2 * 15)

    sends = []

    def copy(src, dst, ssem, rsem, dev):
        return pltpu.make_async_remote_copy(
            src_ref=src, dst_ref=dst, send_sem=ssem, recv_sem=rsem,
            device_id=dev, device_id_type=MESH)

    def start(*args):
        c = copy(*args)
        c.start()
        sends.append(c)

    def block(half, k):
        return pl.ds(pl.multiple_of((half * QUARTERS + k) * NB, NB), NB)

    def tile(p):
        return pl.ds(pl.multiple_of(p * 8, 8), 8)

    def tile_of(half, k, p):
        return pl.ds(pl.multiple_of((half * QUARTERS + k) * NB + p * 8, 8), 8)

    for k in far_first:
        start(own.at[block(1 - core, k)], got0.at[k], s0.at[k], r0.at[k], partner)
    start(e0.at[core], e0.at[core], t0, v0, partner)
    for k in far_first:
        mine = own.at[block(core, k)]
        copy(mine, got0.at[k], s0.at[k], r0.at[k], partner).wait_recv()
        part[k] = mine[...] + got0[k]
        for p in planes:
            start(part.at[k, tile(p)], got1.at[k, me], s1.at[k, p], r1.at[k, me], at_plane(p))
    copy(e0.at[1 - core], e0.at[1 - core], t0, v0, partner).wait_recv()
    e1[me] = e0[0] + e0[1]
    for p in planes:
        start(e1.at[me], e1.at[me], t1.at[p], v1.at[me], at_plane(p))
    for k, group in zip(far_first, peers):
        acc = part[k, tile(me)]
        for p in planes:
            copy(part.at[k, tile(p)], got1.at[k, p], s1.at[k, p], r1.at[k, p], at_plane(p)).wait_recv()
            acc = acc + got1[k, p]
        for d in range(4):
            zout[k * 4 + d] = acc[2 * d:2 * d + 2, :]
        for q in group:
            start(zout.at[q], got2.at[z], s2.at[q], r2.at[z], at_z(q))
    for p in planes:
        copy(e1.at[p], e1.at[p], t1.at[p], v1.at[p], at_plane(p)).wait_recv()
    acc = e1[0]
    for p in range(1, PLANE):
        acc = acc + e1[p]
    e2[z] = acc
    for q in zs:
        start(e2.at[z], e2.at[z], t2.at[q], v2.at[z], at_z(q))
    tot = zout[z]
    for q in reversed(zs):
        copy(zout.at[q], got2.at[q], s2.at[q], r2.at[q], at_z(q)).wait_recv()
        tot = tot + got2[q]
    zall[z] = tot
    for q in zs:
        start(zall.at[z], zall.at[z], s3.at[q], r3.at[z], at_z(q))
    near_first = list(reversed(far_first))
    for k, group in zip(near_first, reversed(peers)):
        for q in group:
            copy(zall.at[q], zall.at[q], s3.at[q], r3.at[q], at_z(q)).wait_recv()
        mine = full.at[tile_of(core, k, me)]
        mine[...] = jnp.concatenate([zall[k * 4 + d] for d in range(4)], axis=0)
        for p in planes:
            start(mine, mine, s4.at[k, p], r4.at[k, me], at_plane(p))
    for q in zs:
        copy(e2.at[q], e2.at[q], t2.at[q], v2.at[q], at_z(q)).wait_recv()
    acc = e2[0]
    for q in range(1, ZN):
        acc = acc + e2[q]
    sum_ref[ROWS:ROWS + EXTRA, :] = acc
    sum_ref[DAMP_ROW:DAMP_ROW + 1, :] = jnp.broadcast_to(held[7][...], (1, NB))
    for k in near_first:
        for p in planes:
            got = full.at[tile_of(core, k, p)]
            copy(got, got, s4.at[k, p], r4.at[k, p], at_plane(p)).wait_recv()
        mine = full.at[block(core, k)]
        start(mine, mine, s5.at[k], r5.at[k], partner)
    for k in near_first:
        got = full.at[block(1 - core, k)]
        copy(got, got, s5.at[k], r5.at[k], partner).wait_recv()
    for c in sends:
        c.wait_send()
    sum_ref[0:ROWS, :] = full[...]


def lane(v, c):
    return jnp.take_along_axis(v, jnp.full((8, NB), c, jnp.int32), axis=1, mode="promise_in_bounds")


def sub(v, r):
    return jnp.broadcast_to(v[r:r + 1, :], (8, NB))


def factor_block(c):
    n = len(c)
    row8 = iota((8, NB), 0)
    col = iota((8, NB), 1)
    ws = []

    for s in range(n):
        base = 8 * s
        tile = (col >= base) & (col < base + 8)
        cb = [lane(c[s], base + m) for m in range(8)]
        t = [[sub(cb[m], i) if i >= m else None for m in range(8)] for i in range(8)]
        own = jnp.where(tile, (row8 + base == col).astype(F32), c[s])
        pa = [sub(own, i) for i in range(8)]
        nx = [lane(c[s + 1], base + m) for m in range(8)] if s + 1 < n else None
        rest = [[lane(c[u], base + m) for m in range(8)] for u in range(s + 2, n)]
        low = [[None] * 8 for _ in range(8)]
        inv = []
        for j in range(0, 8, 2):
            k = j + 1
            a11, a21, a22 = t[j][j], t[k][j], t[k][k]
            det = a11 * a22 - a21 * a21
            r1, r2 = lax.rsqrt(a11), lax.rsqrt(a11 * det)
            g1, g2 = a11 * r2, a21 * r2
            inv += [r1, g1]

            def pair(u, v):
                return u * r1, g1 * v - g2 * u

            low[k][j] = a21 * r1
            for i in range(j + 2, 8):
                low[i][j], low[i][k] = pair(t[i][j], t[i][k])
            for i in range(j + 2, 8):
                for m in range(j + 2, i + 1):
                    t[i][m] = t[i][m] - low[i][j] * low[m][j] - low[i][k] * low[m][k]
            rows = [pa] if nx is None else [pa, nx]
            for v in rows:
                v[j], v[k] = pair(v[j], v[k])
                for i in range(j + 2, 8):
                    v[i] = v[i] - low[i][j] * v[j] - low[i][k] * v[k]
        if s + 1 < n:
            d = [nx[m] * pa[m] for m in range(8)]
            d = ((d[0] + d[1]) + (d[2] + d[3])) + ((d[4] + d[5]) + (d[6] + d[7]))
            c[s + 1] = jnp.where(tile, 0.0, c[s + 1]) - d
        out = pa[0]
        for i in range(1, 8):
            out = jnp.where(row8 == i, pa[i], out)
        ws.append(jnp.where(col < base + 8, out, 0.0))
        if s + 2 < n:
            q = list(pa)
            for m in reversed(range(8)):
                for i in range(m + 1, 8):
                    q[m] = q[m] - low[i][m] * q[i]
                q[m] = q[m] * inv[m]
            for u in range(s + 2, n):
                cu = jnp.where(tile, 0.0, c[u])
                for m in range(8):
                    cu = cu - rest[u - s - 2][m] * q[m]
                c[u] = cu
    return ws


def solve_kernel(x_ref, slope_ref, phi_ref, resid_ref, theta_ref,
                 r_out, theta_out, pred_ref, r_ref, a_ref, w_ref, g_ref, y_ref, sems):
    def put(b):
        rows = pl.ds(b * NB, NB)
        return pltpu.make_async_copy(r_ref.at[rows], r_out.at[rows], sems.at[b])

    inv_total = 1.0 / x_ref[ROWS + 6:ROWS + 7, :]
    same = iota((NB, NB), 0) == iota((NB, NB), 1)
    eye = same.astype(F32) * x_ref[DAMP_ROW:DAMP_ROW + 1, :]
    upper = iota((NB, NB), 0) <= iota((NB, NB), 1)
    for k, (i, j) in enumerate(BLOCKS):
        v = x_ref[k * NB:(k + 1) * NB, :] * inv_total
        if i == j:
            t = jnp.transpose(v)
            low = jnp.where(upper, t, v)
            row = ROWS + 4 + i // 2
            low = jnp.where(same, x_ref[row:row + 1, :] * inv_total, low)
            a_ref[i * NB:(i + 1) * NB, i * NB:(i + 1) * NB] = jnp.where(upper, v, t) + eye
            i, v = i + 1, low + eye
            a_ref[i * NB:(i + 1) * NB, i * NB:(i + 1) * NB] = v
        else:
            a_ref[i * NB:(i + 1) * NB, j * NB:(j + 1) * NB] = v
    for i in range(4):
        for j in range(i):
            r_ref[i * NB:(i + 1) * NB, j * NB:(j + 1) * NB] = jnp.zeros((NB, NB), F32)
        g_ref[i] = x_ref[ROWS + i:ROWS + i + 1, :] * inv_total

    for b in range(4):
        lo, hi = b * NB, (b + 1) * NB
        ws = factor_block([a_ref[lo + 8 * s:lo + 8 * s + 8, lo:hi] for s in range(16)])
        w = jnp.concatenate(ws, axis=0)
        w_ref[b] = w
        y = jnp.sum(w * g_ref[b], axis=1, keepdims=True)
        y_ref[b] = y
        panel = dot(w, a_ref[lo:hi, lo:], NN)
        for c in range(b + 1, 4):
            off = c * NB - lo
            piece = panel[:, off:off + NB]
            a_ref[c * NB:(c + 1) * NB, c * NB:] -= dot(piece, panel[:, off:], TN)
            g_ref[c] = g_ref[c] - jnp.sum(piece * y, axis=0, keepdims=True)
        r_ref[lo:hi, lo:hi] = jnp.where(upper, panel[:, :NB], 0.0)
        if b < 3:
            r_ref[lo:hi, hi:] = panel[:, NB:]
        put(b).start()
    xs = [None] * 4
    for b in reversed(range(4)):
        z = y_ref[b]
        if b < 3:
            d = r_ref[b * NB:(b + 1) * NB, (b + 1) * NB:(b + 2) * NB] * xs[b + 1]
            for c in range(b + 2, 4):
                d = d + r_ref[b * NB:(b + 1) * NB, c * NB:(c + 1) * NB] * xs[c]
            z = z - jnp.sum(d, axis=1, keepdims=True)
        xs[b] = jnp.sum(w_ref[b] * z, axis=0, keepdims=True)
    step_row = -jnp.concatenate(xs, axis=1)
    basis, chans = theta_ref.shape
    own = (iota((basis, PARAMS), 1) & 7) == iota((basis, PARAMS), 0)
    pick = ((iota((PARAMS, chans), 0) >> 3) == iota((PARAMS, chans), 1)).astype(F32)
    step = dot(jnp.where(own, step_row, 0.0), pick, NN)
    theta_out[...] = theta_ref[...] + step
    moved = dot(step, phi_ref[...], TN)
    pred = resid_ref[...] + jnp.sum(slope_ref[...] * moved, axis=0, keepdims=True)
    pred_ref[...] = jnp.concatenate([pred[:, :NB], pred[:, NB:]], axis=0)
    for b in range(4):
        put(b).wait()


THETA_T = True
VM = pl.BlockSpec(memory_space=pltpu.VMEM)


def sds(*shape):
    return jax.ShapeDtypeStruct(shape, F32)


def reduce_call(ysize, *args):
    basis, chans = args[5].shape
    slots = 256
    dma = pltpu.SemaphoreType.DMA
    four, grid, line = dma((QUARTERS,)), dma((QUARTERS, PLANE)), dma((ZN,))
    return pl.pallas_call(
        functools.partial(reduce_kernel, ysize),
        name="reduce",
        out_shape=tuple(pltpu.VMEM(d, F32) for d in ((ROWS + EXTRA, NB), (chans, slots), (basis, slots), (1, slots), (basis, chans))),
        in_specs=[pl.BlockSpec(memory_space=pl.ANY)] * 8,
        out_specs=(VM,) * 5,
        scratch_shapes=[pltpu.VMEM(a.shape, a.dtype) for a in args] + [
            dma((8,)),
            pltpu.VMEM((ROWS, NB), F32),
            pltpu.VMEM((QUARTERS, NB, NB), F32),
            pltpu.VMEM((QUARTERS, NB, NB), F32),
            pltpu.VMEM((QUARTERS, PLANE, 8, NB), F32),
            pltpu.VMEM((ZN, 2, NB), F32),
            pltpu.VMEM((ZN, 2, NB), F32),
            pltpu.VMEM((ZN, 2, NB), F32),
            pltpu.VMEM((ROWS, NB), F32),
            pltpu.VMEM((2, 8, NB), F32),
            pltpu.VMEM((PLANE, 8, NB), F32),
            pltpu.VMEM((ZN, 8, NB), F32),
        ] + [four] * 2 + [grid] * 2 + [line] * 4 + [grid] * 2 + [four] * 2 + [dma] * 2 + [line] * 4,
        compiler_params=pltpu.CompilerParams(collective_id=0, has_side_effects=True),
    )(*args)


def solve_call(summed, slope, phi, resid, theta):
    slots = resid.shape[1]
    return pl.pallas_call(
        solve_kernel,
        name="solve",
        out_shape=(sds(PARAMS, PARAMS), sds(*theta.shape), sds(slots // NB, NB)),
        in_specs=[VM] * 5,
        out_specs=(pl.BlockSpec(memory_space=pl.ANY), VM, VM),
        scratch_shapes=[
            pltpu.VMEM((PARAMS, PARAMS), F32),
            pltpu.VMEM((PARAMS, PARAMS), F32),
            pltpu.VMEM((4, NB, NB), F32),
            pltpu.VMEM((4, 1, NB), F32),
            pltpu.VMEM((4, NB, 1), F32),
            pltpu.SemaphoreType.DMA((4,)),
        ],
        compiler_params=pltpu.CompilerParams(vmem_limit_bytes=24 << 20),
    )(summed, slope, phi, resid, theta)


def on_device(images, gauge_pixel, row_mask, gauge_counts, targets, theta, amplitude, damping):
    def lanes(v):
        return v.reshape(-1, NB)

    terms = reduce_call(
        4, gauge_counts.reshape(1, 1), images.reshape(-1, NB), lanes(gauge_pixel), lanes(row_mask),
        lanes(targets), theta.T, amplitude.reshape(1, -1), damping.reshape(1, 1))
    r, new_theta, pred = solve_call(*terms)
    return r, new_theta.T, pred.reshape(-1)


def solution(mesh):
    return jax.shard_map(
        on_device,
        mesh=mesh,
        in_specs=(P("rows", None, None), P("rows"), P("rows"), P("rows"), P("rows"), P(), P(), P()),
        out_specs=(P(), P(), P(("rows", "cols"))),
        check_vma=False,
    )
```

```python
import functools

import jax
import jax.numpy as jnp
import numpy as np
from jax import lax
from jax.experimental import pallas as pl
from jax.experimental.pallas import tpu as pltpu
from jax.sharding import PartitionSpec as P

HI = lax.Precision.HIGHEST
F32 = jnp.float32
NN = (((1,), (0,)), ((), ()))
NT = (((1,), (1,)), ((), ()))
TN = (((0,), (0,)), ((), ()))
MESH = pl.DeviceIdType.MESH

Y_KIND = [(0, 1.5), (1, 1.5), (0, 1.5), (2, 1.5), (1, 1.5), (0, 1.5), (0, 3.0), (0, 3.0)]
X_KIND = [(0, 1.5), (0, 1.5), (1, 1.5), (0, 1.5), (1, 1.5), (2, 1.5), (0, 3.0), (2, 3.0)]

NB = 128
PARAMS = 512
BLOCKS = [(0, 0), (0, 1), (0, 2), (0, 3), (1, 2), (1, 3), (2, 2), (2, 3)]
PLANE = 16
ZN = 16
QUARTERS = 4
ROWS = len(BLOCKS) * NB
EXTRA = 8
DAMP_ROW = ROWS + EXTRA - 1


def dot(a, b, dims):
    return lax.dot_general(a, b, dims, precision=HI, preferred_element_type=F32)


def parts(v):
    def head(x):
        return x.astype(jnp.bfloat16).astype(F32)

    h = head(v)
    m = head(v - h)
    return h, m, v - h - m


def dot6(a, b, dims):
    da, db = dims[0][0][0], dims[0][1][0]
    ah, am, al = (t.astype(jnp.bfloat16) for t in parts(a))
    bh, bm, bl = (t.astype(jnp.bfloat16) for t in parts(b))
    left = jnp.concatenate([al, am, ah, am, ah, ah], axis=da)
    right = jnp.concatenate([bh, bm, bl, bh, bm, bh], axis=db)
    return lax.dot_general(left, right, dims, preferred_element_type=F32)


def norm_of(order, width):
    t = np.arange(-12, 13).astype(np.float64)
    e = np.exp(-t * t / (2.0 * width * width))
    if order == 1:
        e = -t / width**2 * e
    if order == 2:
        e = (t * t / width**4 - 1.0 / width**2) * e
    return float(1.0 / np.sqrt(np.sum(e * e)))


def filters(t, kinds):
    t2 = t * t
    env = {w: jnp.exp(t2 * (-1.0 / (2.0 * w * w))) for w in sorted({w for _, w in kinds})}
    out = {}
    for order, w in sorted(set(kinds)):
        scale = norm_of(order, w)
        if order == 0:
            out[order, w] = env[w] * scale
        elif order == 1:
            out[order, w] = t * (-scale / w**2) * env[w]
        else:
            out[order, w] = (t2 * (scale / w**4) - scale / w**2) * env[w]
    return out


def iota(shape, dim):
    return lax.broadcasted_iota(jnp.int32, shape, dim)


def local_terms(count_ref, img_ref, pix_ref, mask_ref, targ_ref, theta_ref, amp_ref,
                slope_ref, phi_ref, resid_ref, packed_ref):
    col = lax.axis_index("cols")

    def own(ref):
        v = ref[pl.ds(2 * col, 2), :]
        return jnp.concatenate([v[0:1, :], v[1:2, :]], axis=1)

    pix = own(pix_ref)
    slots = pix.shape[1]
    place = col * slots + iota((1, slots), 1)
    live = ((place < count_ref[...]) & (own(mask_ref) == 1)).astype(F32)

    img = img_ref[...]
    src = iota((img.shape[0], slots), 0)
    row = pix >> 7
    near = (src >> 5) == (row >> 5)
    ty = ((row & 31) - (src & 31)).astype(F32)
    yk = filters(ty, Y_KIND)
    keys = sorted(yk)
    left = jnp.concatenate([jnp.where(near, yk[k], 0.0) for k in keys], axis=1)
    part = dot(img, left, TN)
    tx = ((pix & 127) - iota((img.shape[1], slots), 0)).astype(F32)
    xk = filters(tx, X_KIND)
    phis = []
    for ky, kx in zip(Y_KIND, X_KIND):
        at = keys.index(ky) * slots
        phis.append(jnp.sum(part[:, at:at + slots] * xk[kx], axis=0, keepdims=True))
    phi = jnp.concatenate(phis, axis=0)
    phi_ref[...] = phi

    act = jnp.tanh(dot(theta_ref[...], phi, TN))
    amp = jnp.transpose(jnp.broadcast_to(amp_ref[...], (NB, amp_ref.shape[1])))[:, 0:1]
    resid = live * (jnp.sum(amp * act, axis=0, keepdims=True) - own(targ_ref))
    resid_ref[...] = resid
    slope = live * amp * (1.0 - act * act)
    slope_ref[...] = slope
    jac = jnp.concatenate([slope[c:c + 1, :] * phi for c in range(slope.shape[0])], axis=0)

    upper = iota((NB, NB), 0) <= iota((NB, NB), 1)
    diag = iota((NB, NB), 0) == iota((NB, NB), 1)
    rows = []
    for i in range(4):
        wide = dot(jac[i * NB:(i + 1) * NB], jac[i * NB:], NT)
        for j in range(i, 4):
            block = wide[:, (j - i) * NB:(j - i + 1) * NB]
            if i == j and i % 2 == 0:
                first = block
                continue
            at = BLOCKS.index((i - 1, i - 1) if i == j else (i, j)) * NB
            if i == j:
                rows.append(jnp.sum(jnp.where(diag, block, 0.0), axis=0, keepdims=True))
                block = jnp.where(upper, first, block)
            packed_ref[at:at + NB, :] = block
    grad = dot(jnp.broadcast_to(resid, (8, slots)), jac, NT)
    total = jnp.sum(live, axis=1, keepdims=True)
    rows = [grad[0:1, i * NB:(i + 1) * NB] for i in range(4)] + rows
    rows += [jnp.broadcast_to(total, (1, NB)), jnp.zeros((1, NB), F32)]
    return jnp.concatenate(rows, axis=0)


def reduce_kernel(ysize, *refs):
    args, held, in_sems = refs[:8], refs[13:21], refs[21]
    sum_ref, slope_ref, phi_ref, resid_ref, theta_out = refs[8:13]
    refs = refs[22:]
    own, got0, part, got1, zout, got2, zall, full, e0, e1, e2 = refs[:11]
    (s0, r0), (s1, r1), (s2, r2), (s3, r3), (s4, r4), (s5, r5) = zip(refs[11:23:2], refs[12:23:2])
    (t0, v0), (t1, v1), (t2, v2) = zip(refs[23::2], refs[24::2])
    row = lax.axis_index("rows")
    col = lax.axis_index("cols")
    y, z = row // ZN, lax.rem(row, ZN)
    x, core = col // 2, lax.rem(col, 2)
    me = x * ysize + y
    near = z // QUARTERS
    far_first = [lax.rem(near + d, QUARTERS) for d in (2, 1, 3, 0)]

    def at_plane(p):
        return {"rows": lax.rem(p, ysize) * ZN + z, "cols": (p // ysize) * 2 + core}

    def at_z(q):
        return {"rows": y * ZN + q, "cols": col}

    partner = {"rows": row, "cols": x * 2 + 1 - core}
    shifts = [(i, j) for i in range(PLANE // ysize) for j in range(ysize)][1:]
    shifts.sort(key=lambda d: -min(d[0], PLANE // ysize - d[0]) - min(d[1], ysize - d[1]))
    planes = [
        lax.rem(x + i, PLANE // ysize) * ysize + lax.rem(y + j, ysize) for i, j in shifts]
    peers = [[k * 4 + d for d in range(4)] for k in far_first[:3]]
    peers.append([near * 4 + lax.rem(z + d, 4) for d in range(1, 4)])
    zs = [q for group in peers for q in group]

    loads = [pltpu.make_async_copy(a, h, in_sems.at[i]) for i, (a, h) in enumerate(zip(args, held))]
    for c in loads:
        c.start()

    barrier = pltpu.get_barrier_semaphore()
    for dev in [partner] + [at_plane(p) for p in planes] + [at_z(q) for q in zs]:
        pl.semaphore_signal(barrier, inc=1, device_id=dev, device_id_type=MESH)

    for c in loads:
        c.wait()
    theta_out[...] = held[5][...]
    e0[core] = local_terms(*held[:7], slope_ref, phi_ref, resid_ref, own)

    pl.semaphore_wait(barrier, 1 + 2 * 15)

    sends = []

    def copy(src, dst, ssem, rsem, dev):
        return pltpu.make_async_remote_copy(
            src_ref=src, dst_ref=dst, send_sem=ssem, recv_sem=rsem,
            device_id=dev, device_id_type=MESH)

    def start(*args):
        c = copy(*args)
        c.start()
        sends.append(c)

    def block(half, k):
        return pl.ds(pl.multiple_of((half * QUARTERS + k) * NB, NB), NB)

    def tile(p):
        return pl.ds(pl.multiple_of(p * 8, 8), 8)

    def tile_of(half, k, p):
        return pl.ds(pl.multiple_of((half * QUARTERS + k) * NB + p * 8, 8), 8)

    for k in far_first:
        start(own.at[block(1 - core, k)], got0.at[k], s0.at[k], r0.at[k], partner)
    start(e0.at[core], e0.at[core], t0, v0, partner)
    for k in far_first:
        mine = own.at[block(core, k)]
        copy(mine, got0.at[k], s0.at[k], r0.at[k], partner).wait_recv()
        part[k] = mine[...] + got0[k]
        for p in planes:
            start(part.at[k, tile(p)], got1.at[k, me], s1.at[k, p], r1.at[k, me], at_plane(p))
    copy(e0.at[1 - core], e0.at[1 - core], t0, v0, partner).wait_recv()
    e1[me] = e0[0] + e0[1]
    for p in planes:
        start(e1.at[me], e1.at[me], t1.at[p], v1.at[me], at_plane(p))
    for k, group in zip(far_first, peers):
        acc = part[k, tile(me)]
        for p in planes:
            copy(part.at[k, tile(p)], got1.at[k, p], s1.at[k, p], r1.at[k, p], at_plane(p)).wait_recv()
            acc = acc + got1[k, p]
        for d in range(4):
            zout[k * 4 + d] = acc[2 * d:2 * d + 2, :]
        for q in group:
            start(zout.at[q], got2.at[z], s2.at[q], r2.at[z], at_z(q))
    for p in planes:
        copy(e1.at[p], e1.at[p], t1.at[p], v1.at[p], at_plane(p)).wait_recv()
    acc = e1[0]
    for p in range(1, PLANE):
        acc = acc + e1[p]
    e2[z] = acc
    for q in zs:
        start(e2.at[z], e2.at[z], t2.at[q], v2.at[z], at_z(q))
    tot = zout[z]
    for q in reversed(zs):
        copy(zout.at[q], got2.at[q], s2.at[q], r2.at[q], at_z(q)).wait_recv()
        tot = tot + got2[q]
    zall[z] = tot
    for q in zs:
        start(zall.at[z], zall.at[z], s3.at[q], r3.at[z], at_z(q))
    near_first = list(reversed(far_first))
    for k, group in zip(near_first, reversed(peers)):
        for q in group:
            copy(zall.at[q], zall.at[q], s3.at[q], r3.at[q], at_z(q)).wait_recv()
        mine = full.at[tile_of(core, k, me)]
        mine[...] = jnp.concatenate([zall[k * 4 + d] for d in range(4)], axis=0)
        for p in planes:
            start(mine, mine, s4.at[k, p], r4.at[k, me], at_plane(p))
    for q in zs:
        copy(e2.at[q], e2.at[q], t2.at[q], v2.at[q], at_z(q)).wait_recv()
    acc = e2[0]
    for q in range(1, ZN):
        acc = acc + e2[q]
    sum_ref[ROWS:ROWS + EXTRA, :] = acc
    sum_ref[DAMP_ROW:DAMP_ROW + 1, :] = jnp.broadcast_to(held[7][...], (1, NB))
    for k in near_first:
        for p in planes:
            got = full.at[tile_of(core, k, p)]
            copy(got, got, s4.at[k, p], r4.at[k, p], at_plane(p)).wait_recv()
        mine = full.at[block(core, k)]
        start(mine, mine, s5.at[k], r5.at[k], partner)
    for k in near_first:
        got = full.at[block(1 - core, k)]
        copy(got, got, s5.at[k], r5.at[k], partner).wait_recv()
    for c in sends:
        c.wait_send()
    sum_ref[0:ROWS, :] = full[...]


def lane(v, c):
    return jnp.take_along_axis(v, jnp.full((8, NB), c, jnp.int32), axis=1, mode="promise_in_bounds")


def sub(v, r):
    return jnp.broadcast_to(v[r:r + 1, :], (8, NB))


def factor_block(c):
    n = len(c)
    row8 = iota((8, NB), 0)
    col = iota((8, NB), 1)
    ws = []

    for s in range(n):
        base = 8 * s
        tile = (col >= base) & (col < base + 8)
        cb = [lane(c[s], base + m) for m in range(8)]
        t = [[sub(cb[m], i) if i >= m else None for m in range(8)] for i in range(8)]
        own = jnp.where(tile, (row8 + base == col).astype(F32), c[s])
        pa = [sub(own, i) for i in range(8)]
        nx = [lane(c[s + 1], base + m) for m in range(8)] if s + 1 < n else None
        rest = [[lane(c[u], base + m) for m in range(8)] for u in range(s + 2, n)]
        low = [[None] * 8 for _ in range(8)]
        inv = []
        for j in range(0, 8, 2):
            k = j + 1
            a11, a21, a22 = t[j][j], t[k][j], t[k][k]
            det = a11 * a22 - a21 * a21
            r1, r2 = lax.rsqrt(a11), lax.rsqrt(a11 * det)
            g1, g2 = a11 * r2, a21 * r2
            inv += [r1, g1]

            def pair(u, v):
                return u * r1, g1 * v - g2 * u

            low[k][j] = a21 * r1
            for i in range(j + 2, 8):
                low[i][j], low[i][k] = pair(t[i][j], t[i][k])
            for i in range(j + 2, 8):
                for m in range(j + 2, i + 1):
                    t[i][m] = t[i][m] - low[i][j] * low[m][j] - low[i][k] * low[m][k]
            rows = [pa] if nx is None else [pa, nx]
            for v in rows:
                v[j], v[k] = pair(v[j], v[k])
                for i in range(j + 2, 8):
                    v[i] = v[i] - low[i][j] * v[j] - low[i][k] * v[k]
        if s + 1 < n:
            d = [nx[m] * pa[m] for m in range(8)]
            d = ((d[0] + d[1]) + (d[2] + d[3])) + ((d[4] + d[5]) + (d[6] + d[7]))
            c[s + 1] = jnp.where(tile, 0.0, c[s + 1]) - d
        out = pa[0]
        for i in range(1, 8):
            out = jnp.where(row8 == i, pa[i], out)
        ws.append(jnp.where(col < base + 8, out, 0.0))
        if s + 2 < n:
            q = list(pa)
            for m in reversed(range(8)):
                for i in range(m + 1, 8):
                    q[m] = q[m] - low[i][m] * q[i]
                q[m] = q[m] * inv[m]
            for u in range(s + 2, n):
                cu = jnp.where(tile, 0.0, c[u])
                for m in range(8):
                    cu = cu - rest[u - s - 2][m] * q[m]
                c[u] = cu
    return ws


def solve_kernel(x_ref, slope_ref, phi_ref, resid_ref, theta_ref,
                 r_out, theta_out, pred_ref, r_ref, a_ref, w_ref, g_ref, y_ref, sems):
    def put(b):
        rows = pl.ds(b * NB, NB)
        return pltpu.make_async_copy(r_ref.at[rows], r_out.at[rows], sems.at[b])

    inv_total = 1.0 / x_ref[ROWS + 6:ROWS + 7, :]
    same = iota((NB, NB), 0) == iota((NB, NB), 1)
    eye = same.astype(F32) * x_ref[DAMP_ROW:DAMP_ROW + 1, :]
    upper = iota((NB, NB), 0) <= iota((NB, NB), 1)
    for k, (i, j) in enumerate(BLOCKS):
        v = x_ref[k * NB:(k + 1) * NB, :] * inv_total
        if i == j:
            t = jnp.transpose(v)
            low = jnp.where(upper, t, v)
            row = ROWS + 4 + i // 2
            low = jnp.where(same, x_ref[row:row + 1, :] * inv_total, low)
            a_ref[i * NB:(i + 1) * NB, i * NB:(i + 1) * NB] = jnp.where(upper, v, t) + eye
            i, v = i + 1, low + eye
            a_ref[i * NB:(i + 1) * NB, i * NB:(i + 1) * NB] = v
        else:
            a_ref[i * NB:(i + 1) * NB, j * NB:(j + 1) * NB] = v
    for i in range(4):
        for j in range(i):
            r_ref[i * NB:(i + 1) * NB, j * NB:(j + 1) * NB] = jnp.zeros((NB, NB), F32)
        g_ref[i] = x_ref[ROWS + i:ROWS + i + 1, :] * inv_total

    for b in range(4):
        lo, hi = b * NB, (b + 1) * NB
        ws = factor_block([a_ref[lo + 8 * s:lo + 8 * s + 8, lo:hi] for s in range(16)])
        w = jnp.concatenate(ws, axis=0)
        w_ref[b] = w
        y = jnp.sum(w * g_ref[b], axis=1, keepdims=True)
        y_ref[b] = y
        panel = dot6(w, a_ref[lo:hi, lo:], NN)
        for c in range(b + 1, 4):
            off = c * NB - lo
            piece = panel[:, off:off + NB]
            a_ref[c * NB:(c + 1) * NB, c * NB:] -= dot6(piece, panel[:, off:], TN)
            g_ref[c] = g_ref[c] - jnp.sum(piece * y, axis=0, keepdims=True)
        r_ref[lo:hi, lo:hi] = jnp.where(upper, panel[:, :NB], 0.0)
        if b < 3:
            r_ref[lo:hi, hi:] = panel[:, NB:]
        put(b).start()
    xs = [None] * 4
    for b in reversed(range(4)):
        z = y_ref[b]
        if b < 3:
            d = r_ref[b * NB:(b + 1) * NB, (b + 1) * NB:(b + 2) * NB] * xs[b + 1]
            for c in range(b + 2, 4):
                d = d + r_ref[b * NB:(b + 1) * NB, c * NB:(c + 1) * NB] * xs[c]
            z = z - jnp.sum(d, axis=1, keepdims=True)
        xs[b] = jnp.sum(w_ref[b] * z, axis=0, keepdims=True)
    step_row = -jnp.concatenate(xs, axis=1)
    basis, chans = theta_ref.shape
    own = (iota((basis, PARAMS), 1) & 7) == iota((basis, PARAMS), 0)
    pick = ((iota((PARAMS, chans), 0) >> 3) == iota((PARAMS, chans), 1)).astype(jnp.bfloat16)
    rows = [jnp.where(own, t, 0.0).astype(jnp.bfloat16) for t in parts(step_row)]
    three = lax.dot_general(
        jnp.concatenate(rows[::-1], axis=0), pick, NN, preferred_element_type=F32)
    step = three[:basis] + three[basis:2 * basis] + three[2 * basis:]
    theta_out[...] = theta_ref[...] + step
    moved = dot(step, phi_ref[...], TN)
    pred = resid_ref[...] + jnp.sum(slope_ref[...] * moved, axis=0, keepdims=True)
    pred_ref[...] = jnp.concatenate([pred[:, :NB], pred[:, NB:]], axis=0)
    for b in range(4):
        put(b).wait()


THETA_T = True
VM = pl.BlockSpec(memory_space=pltpu.VMEM)


def sds(*shape):
    return jax.ShapeDtypeStruct(shape, F32)


def reduce_call(ysize, *args):
    basis, chans = args[5].shape
    slots = 256
    dma = pltpu.SemaphoreType.DMA
    four, grid, line = dma((QUARTERS,)), dma((QUARTERS, PLANE)), dma((ZN,))
    return pl.pallas_call(
        functools.partial(reduce_kernel, ysize),
        name="reduce",
        out_shape=tuple(pltpu.VMEM(d, F32) for d in ((ROWS + EXTRA, NB), (chans, slots), (basis, slots), (1, slots), (basis, chans))),
        in_specs=[pl.BlockSpec(memory_space=pl.ANY)] * 8,
        out_specs=(VM,) * 5,
        scratch_shapes=[pltpu.VMEM(a.shape, a.dtype) for a in args] + [
            dma((8,)),
            pltpu.VMEM((ROWS, NB), F32),
            pltpu.VMEM((QUARTERS, NB, NB), F32),
            pltpu.VMEM((QUARTERS, NB, NB), F32),
            pltpu.VMEM((QUARTERS, PLANE, 8, NB), F32),
            pltpu.VMEM((ZN, 2, NB), F32),
            pltpu.VMEM((ZN, 2, NB), F32),
            pltpu.VMEM((ZN, 2, NB), F32),
            pltpu.VMEM((ROWS, NB), F32),
            pltpu.VMEM((2, 8, NB), F32),
            pltpu.VMEM((PLANE, 8, NB), F32),
            pltpu.VMEM((ZN, 8, NB), F32),
        ] + [four] * 2 + [grid] * 2 + [line] * 4 + [grid] * 2 + [four] * 2 + [dma] * 2 + [line] * 4,
        compiler_params=pltpu.CompilerParams(collective_id=0, has_side_effects=True),
    )(*args)


def solve_call(summed, slope, phi, resid, theta):
    slots = resid.shape[1]
    return pl.pallas_call(
        solve_kernel,
        name="solve",
        out_shape=(sds(PARAMS, PARAMS), sds(*theta.shape), sds(slots // NB, NB)),
        in_specs=[VM] * 5,
        out_specs=(pl.BlockSpec(memory_space=pl.ANY), VM, VM),
        scratch_shapes=[
            pltpu.VMEM((PARAMS, PARAMS), F32),
            pltpu.VMEM((PARAMS, PARAMS), F32),
            pltpu.VMEM((4, NB, NB), F32),
            pltpu.VMEM((4, 1, NB), F32),
            pltpu.VMEM((4, NB, 1), F32),
            pltpu.SemaphoreType.DMA((4,)),
        ],
        compiler_params=pltpu.CompilerParams(vmem_limit_bytes=24 << 20),
    )(summed, slope, phi, resid, theta)


def on_device(images, gauge_pixel, row_mask, gauge_counts, targets, theta, amplitude, damping):
    def lanes(v):
        return v.reshape(-1, NB)

    terms = reduce_call(
        4, gauge_counts.reshape(1, 1), images.reshape(-1, NB), lanes(gauge_pixel), lanes(row_mask),
        lanes(targets), theta.T, amplitude.reshape(1, -1), damping.reshape(1, 1))
    r, new_theta, pred = solve_call(*terms)
    return r, new_theta.T, pred.reshape(-1)


def solution(mesh):
    return jax.shard_map(
        on_device,
        mesh=mesh,
        in_specs=(P("rows", None, None), P("rows"), P("rows"), P("rows"), P("rows"), P(), P(), P()),
        out_specs=(P(), P(), P(("rows", "cols"))),
        check_vma=False,
    )
```

```python
import functools

import jax
import jax.numpy as jnp
import numpy as np
from jax import lax
from jax.experimental import pallas as pl
from jax.experimental.pallas import tpu as pltpu
from jax.sharding import PartitionSpec as P

HI = lax.Precision.HIGHEST
F32 = jnp.float32
NN = (((1,), (0,)), ((), ()))
NT = (((1,), (1,)), ((), ()))
TN = (((0,), (0,)), ((), ()))
MESH = pl.DeviceIdType.MESH

Y_KIND = [(0, 1.5), (1, 1.5), (0, 1.5), (2, 1.5), (1, 1.5), (0, 1.5), (0, 3.0), (0, 3.0)]
X_KIND = [(0, 1.5), (0, 1.5), (1, 1.5), (0, 1.5), (1, 1.5), (2, 1.5), (0, 3.0), (2, 3.0)]

NB = 128
PARAMS = 512
BLOCKS = [(0, 0), (0, 1), (0, 2), (0, 3), (1, 2), (1, 3), (2, 2), (2, 3)]
PLANE = 16
ZN = 16
QUARTERS = 4
ROWS = len(BLOCKS) * NB
EXTRA = 8
DAMP_ROW = ROWS + EXTRA - 1


def dot(a, b, dims):
    return lax.dot_general(a, b, dims, precision=HI, preferred_element_type=F32)


def parts(v):
    def head(x):
        return x.astype(jnp.bfloat16).astype(F32)

    h = head(v)
    m = head(v - h)
    return h, m, v - h - m


def dot6(a, b, dims):
    da, db = dims[0][0][0], dims[0][1][0]
    ah, am, al = (t.astype(jnp.bfloat16) for t in parts(a))
    bh, bm, bl = (t.astype(jnp.bfloat16) for t in parts(b))
    left = jnp.concatenate([al, am, ah, am, ah, ah], axis=da)
    right = jnp.concatenate([bh, bm, bl, bh, bm, bh], axis=db)
    return lax.dot_general(left, right, dims, preferred_element_type=F32)


def norm_of(order, width):
    t = np.arange(-12, 13).astype(np.float64)
    e = np.exp(-t * t / (2.0 * width * width))
    if order == 1:
        e = -t / width**2 * e
    if order == 2:
        e = (t * t / width**4 - 1.0 / width**2) * e
    return float(1.0 / np.sqrt(np.sum(e * e)))


def filters(t, kinds):
    t2 = t * t
    env = {w: jnp.exp(t2 * (-1.0 / (2.0 * w * w))) for w in sorted({w for _, w in kinds})}
    out = {}
    for order, w in sorted(set(kinds)):
        scale = norm_of(order, w)
        if order == 0:
            out[order, w] = env[w] * scale
        elif order == 1:
            out[order, w] = t * (-scale / w**2) * env[w]
        else:
            out[order, w] = (t2 * (scale / w**4) - scale / w**2) * env[w]
    return out


def iota(shape, dim):
    return lax.broadcasted_iota(jnp.int32, shape, dim)


def local_terms(count_ref, img_ref, pix_ref, mask_ref, targ_ref, theta_ref, amp_ref,
                slope_ref, phi_ref, resid_ref, packed_ref):
    col = lax.axis_index("cols")

    def own(ref):
        v = ref[pl.ds(2 * col, 2), :]
        return jnp.concatenate([v[0:1, :], v[1:2, :]], axis=1)

    pix = own(pix_ref)
    slots = pix.shape[1]
    place = col * slots + iota((1, slots), 1)
    live = ((place < count_ref[...]) & (own(mask_ref) == 1)).astype(F32)

    img = img_ref[...]
    src = iota((img.shape[0], slots), 0)
    row = pix >> 7
    near = (src >> 5) == (row >> 5)
    ty = ((row & 31) - (src & 31)).astype(F32)
    yk = filters(ty, Y_KIND)
    keys = sorted(yk)
    left = jnp.concatenate([jnp.where(near, yk[k], 0.0) for k in keys], axis=1)
    part = dot(img, left, TN)
    tx = ((pix & 127) - iota((img.shape[1], slots), 0)).astype(F32)
    xk = filters(tx, X_KIND)
    phis = []
    for ky, kx in zip(Y_KIND, X_KIND):
        at = keys.index(ky) * slots
        phis.append(jnp.sum(part[:, at:at + slots] * xk[kx], axis=0, keepdims=True))
    phi = jnp.concatenate(phis, axis=0)
    phi_ref[...] = phi

    act = jnp.tanh(dot(theta_ref[...], phi, TN))
    amp = jnp.transpose(jnp.broadcast_to(amp_ref[...], (NB, amp_ref.shape[1])))[:, 0:1]
    resid = live * (jnp.sum(amp * act, axis=0, keepdims=True) - own(targ_ref))
    resid_ref[...] = resid
    slope = live * amp * (1.0 - act * act)
    slope_ref[...] = slope
    jac = jnp.concatenate([slope[c:c + 1, :] * phi for c in range(slope.shape[0])], axis=0)

    upper = iota((NB, NB), 0) <= iota((NB, NB), 1)
    diag = iota((NB, NB), 0) == iota((NB, NB), 1)
    rows = []
    for i in range(4):
        wide = dot(jac[i * NB:(i + 1) * NB], jac[i * NB:], NT)
        for j in range(i, 4):
            block = wide[:, (j - i) * NB:(j - i + 1) * NB]
            if i == j and i % 2 == 0:
                first = block
                continue
            at = BLOCKS.index((i - 1, i - 1) if i == j else (i, j)) * NB
            if i == j:
                rows.append(jnp.sum(jnp.where(diag, block, 0.0), axis=0, keepdims=True))
                block = jnp.where(upper, first, block)
            packed_ref[at:at + NB, :] = block
    grad = dot(jnp.broadcast_to(resid, (8, slots)), jac, NT)
    total = jnp.sum(live, axis=1, keepdims=True)
    rows = [grad[0:1, i * NB:(i + 1) * NB] for i in range(4)] + rows
    rows += [jnp.broadcast_to(total, (1, NB)), jnp.zeros((1, NB), F32)]
    return jnp.concatenate(rows, axis=0)


def reduce_kernel(ysize, *refs):
    args, held, in_sems = refs[:8], refs[13:21], refs[21]
    sum_ref, slope_ref, phi_ref, resid_ref, theta_out = refs[8:13]
    refs = refs[22:]
    own, got0, part, got1, zout, got2, zall, full, e0, e1, e2 = refs[:11]
    (s0, r0), (s1, r1), (s2, r2), (s3, r3), (s4, r4), (s5, r5) = zip(refs[11:23:2], refs[12:23:2])
    (t0, v0), (t1, v1), (t2, v2) = zip(refs[23::2], refs[24::2])
    row = lax.axis_index("rows")
    col = lax.axis_index("cols")
    y, z = row // ZN, lax.rem(row, ZN)
    x, core = col // 2, lax.rem(col, 2)
    me = x * ysize + y
    near = z // QUARTERS
    far_first = [lax.rem(near + d, QUARTERS) for d in (2, 1, 3, 0)]

    def at_plane(p):
        return {"rows": lax.rem(p, ysize) * ZN + z, "cols": (p // ysize) * 2 + core}

    def at_z(q):
        return {"rows": y * ZN + q, "cols": col}

    partner = {"rows": row, "cols": x * 2 + 1 - core}
    shifts = [(i, j) for i in range(PLANE // ysize) for j in range(ysize)][1:]
    shifts.sort(key=lambda d: -min(d[0], PLANE // ysize - d[0]) - min(d[1], ysize - d[1]))
    planes = [
        lax.rem(x + i, PLANE // ysize) * ysize + lax.rem(y + j, ysize) for i, j in shifts]
    peers = [[k * 4 + d for d in range(4)] for k in far_first[:3]]
    peers.append([near * 4 + lax.rem(z + d, 4) for d in range(1, 4)])
    zs = [q for group in peers for q in group]

    loads = [pltpu.make_async_copy(a, h, in_sems.at[i]) for i, (a, h) in enumerate(zip(args, held))]
    for c in loads:
        c.start()

    barrier = pltpu.get_barrier_semaphore()
    for dev in [partner] + [at_plane(p) for p in planes] + [at_z(q) for q in zs]:
        pl.semaphore_signal(barrier, inc=1, device_id=dev, device_id_type=MESH)

    for c in loads:
        c.wait()
    theta_out[...] = held[5][...]
    e0[core] = local_terms(*held[:7], slope_ref, phi_ref, resid_ref, own)

    pl.semaphore_wait(barrier, 1 + 2 * 15)

    sends = []

    def copy(src, dst, ssem, rsem, dev):
        return pltpu.make_async_remote_copy(
            src_ref=src, dst_ref=dst, send_sem=ssem, recv_sem=rsem,
            device_id=dev, device_id_type=MESH)

    def start(*args):
        c = copy(*args)
        c.start()
        sends.append(c)

    def block(half, k):
        return pl.ds(pl.multiple_of((half * QUARTERS + k) * NB, NB), NB)

    def tile(p):
        return pl.ds(pl.multiple_of(p * 8, 8), 8)

    def tile_of(half, k, p):
        return pl.ds(pl.multiple_of((half * QUARTERS + k) * NB + p * 8, 8), 8)

    for k in far_first:
        start(own.at[block(1 - core, k)], got0.at[k], s0.at[k], r0.at[k], partner)
    start(e0.at[core], e0.at[core], t0, v0, partner)
    for k in far_first:
        mine = own.at[block(core, k)]
        copy(mine, got0.at[k], s0.at[k], r0.at[k], partner).wait_recv()
        part[k] = mine[...] + got0[k]
        for p in planes:
            start(part.at[k, tile(p)], got1.at[k, me], s1.at[k, p], r1.at[k, me], at_plane(p))
    copy(e0.at[1 - core], e0.at[1 - core], t0, v0, partner).wait_recv()
    e1[me] = e0[0] + e0[1]
    for p in planes:
        start(e1.at[me], e1.at[me], t1.at[p], v1.at[me], at_plane(p))
    for k, group in zip(far_first, peers):
        acc = part[k, tile(me)]
        for p in planes:
            copy(part.at[k, tile(p)], got1.at[k, p], s1.at[k, p], r1.at[k, p], at_plane(p)).wait_recv()
            acc = acc + got1[k, p]
        for d in range(4):
            zout[k * 4 + d] = acc[2 * d:2 * d + 2, :]
        for q in group:
            start(zout.at[q], got2.at[z], s2.at[q], r2.at[z], at_z(q))
    for p in planes:
        copy(e1.at[p], e1.at[p], t1.at[p], v1.at[p], at_plane(p)).wait_recv()
    acc = e1[0]
    for p in range(1, PLANE):
        acc = acc + e1[p]
    e2[z] = acc
    for q in zs:
        start(e2.at[z], e2.at[z], t2.at[q], v2.at[z], at_z(q))
    tot = zout[z]
    for q in reversed(zs):
        copy(zout.at[q], got2.at[q], s2.at[q], r2.at[q], at_z(q)).wait_recv()
        tot = tot + got2[q]
    zall[z] = tot
    for q in zs:
        start(zall.at[z], zall.at[z], s3.at[q], r3.at[z], at_z(q))
    early = len(sends)
    near_first = list(reversed(far_first))
    for k, group in zip(near_first, reversed(peers)):
        for q in group:
            copy(zall.at[q], zall.at[q], s3.at[q], r3.at[q], at_z(q)).wait_recv()
        mine = full.at[tile_of(core, k, me)]
        mine[...] = jnp.concatenate([zall[k * 4 + d] for d in range(4)], axis=0)
        for p in planes:
            start(mine, mine, s4.at[k, p], r4.at[k, me], at_plane(p))
    for q in zs:
        copy(e2.at[q], e2.at[q], t2.at[q], v2.at[q], at_z(q)).wait_recv()
    acc = e2[0]
    for q in range(1, ZN):
        acc = acc + e2[q]
    for c in sends[:early]:
        c.wait_send()
    sum_ref[ROWS:ROWS + EXTRA, :] = acc
    sum_ref[DAMP_ROW:DAMP_ROW + 1, :] = jnp.broadcast_to(held[7][...], (1, NB))
    for k in near_first:
        for p in planes:
            got = full.at[tile_of(core, k, p)]
            copy(got, got, s4.at[k, p], r4.at[k, p], at_plane(p)).wait_recv()
        mine = full.at[block(core, k)]
        start(mine, mine, s5.at[k], r5.at[k], partner)
        sum_ref[block(core, k), :] = mine[...]
    for c in sends[early:]:
        c.wait_send()
    for k in near_first:
        got = full.at[block(1 - core, k)]
        copy(got, got, s5.at[k], r5.at[k], partner).wait_recv()
        sum_ref[block(1 - core, k), :] = got[...]


def lane(v, c):
    return jnp.take_along_axis(v, jnp.full((8, NB), c, jnp.int32), axis=1, mode="promise_in_bounds")


def sub(v, r):
    return jnp.broadcast_to(v[r:r + 1, :], (8, NB))


def factor_block(c):
    n = len(c)
    row8 = iota((8, NB), 0)
    col = iota((8, NB), 1)
    ws = []

    for s in range(n):
        base = 8 * s
        tile = (col >= base) & (col < base + 8)
        cb = [lane(c[s], base + m) for m in range(8)]
        t = [[sub(cb[m], i) if i >= m else None for m in range(8)] for i in range(8)]
        own = jnp.where(tile, (row8 + base == col).astype(F32), c[s])
        pa = [sub(own, i) for i in range(8)]
        nx = [lane(c[s + 1], base + m) for m in range(8)] if s + 1 < n else None
        rest = [[lane(c[u], base + m) for m in range(8)] for u in range(s + 2, n)]
        low = [[None] * 8 for _ in range(8)]
        inv = []
        for j in range(0, 8, 2):
            k = j + 1
            a11, a21, a22 = t[j][j], t[k][j], t[k][k]
            det = a11 * a22 - a21 * a21
            r1, r2 = lax.rsqrt(a11), lax.rsqrt(a11 * det)
            g1, g2 = a11 * r2, a21 * r2
            inv += [r1, g1]

            def pair(u, v):
                return u * r1, g1 * v - g2 * u

            low[k][j] = a21 * r1
            for i in range(j + 2, 8):
                low[i][j], low[i][k] = pair(t[i][j], t[i][k])
            for i in range(j + 2, 8):
                for m in range(j + 2, i + 1):
                    t[i][m] = t[i][m] - low[i][j] * low[m][j] - low[i][k] * low[m][k]
            rows = [pa] if nx is None else [pa, nx]
            for v in rows:
                v[j], v[k] = pair(v[j], v[k])
                for i in range(j + 2, 8):
                    v[i] = v[i] - low[i][j] * v[j] - low[i][k] * v[k]
        if s + 1 < n:
            d = [nx[m] * pa[m] for m in range(8)]
            d = ((d[0] + d[1]) + (d[2] + d[3])) + ((d[4] + d[5]) + (d[6] + d[7]))
            c[s + 1] = jnp.where(tile, 0.0, c[s + 1]) - d
        out = pa[0]
        for i in range(1, 8):
            out = jnp.where(row8 == i, pa[i], out)
        ws.append(jnp.where(col < base + 8, out, 0.0))
        if s + 2 < n:
            q = list(pa)
            for m in reversed(range(8)):
                for i in range(m + 1, 8):
                    q[m] = q[m] - low[i][m] * q[i]
                q[m] = q[m] * inv[m]
            for u in range(s + 2, n):
                cu = jnp.where(tile, 0.0, c[u])
                for m in range(8):
                    cu = cu - rest[u - s - 2][m] * q[m]
                c[u] = cu
    return ws


def solve_kernel(x_ref, slope_ref, phi_ref, resid_ref, theta_ref,
                 r_out, theta_out, pred_ref, r_ref, a_ref, w_ref, g_ref, y_ref, sems):
    def put(b):
        rows = pl.ds(b * NB, NB)
        return pltpu.make_async_copy(r_ref.at[rows], r_out.at[rows], sems.at[b])

    inv_total = 1.0 / x_ref[ROWS + 6:ROWS + 7, :]
    same = iota((NB, NB), 0) == iota((NB, NB), 1)
    eye = same.astype(F32) * x_ref[DAMP_ROW:DAMP_ROW + 1, :]
    upper = iota((NB, NB), 0) <= iota((NB, NB), 1)
    for k, (i, j) in enumerate(BLOCKS):
        v = x_ref[k * NB:(k + 1) * NB, :] * inv_total
        if i == j:
            t = jnp.transpose(v)
            low = jnp.where(upper, t, v)
            row = ROWS + 4 + i // 2
            low = jnp.where(same, x_ref[row:row + 1, :] * inv_total, low)
            a_ref[i * NB:(i + 1) * NB, i * NB:(i + 1) * NB] = jnp.where(upper, v, t) + eye
            i, v = i + 1, low + eye
            a_ref[i * NB:(i + 1) * NB, i * NB:(i + 1) * NB] = v
        else:
            a_ref[i * NB:(i + 1) * NB, j * NB:(j + 1) * NB] = v
    for i in range(4):
        for j in range(i):
            r_ref[i * NB:(i + 1) * NB, j * NB:(j + 1) * NB] = jnp.zeros((NB, NB), F32)
        g_ref[i] = x_ref[ROWS + i:ROWS + i + 1, :] * inv_total

    for b in range(4):
        lo, hi = b * NB, (b + 1) * NB
        ws = factor_block([a_ref[lo + 8 * s:lo + 8 * s + 8, lo:hi] for s in range(16)])
        w = jnp.concatenate(ws, axis=0)
        w_ref[b] = w
        y = jnp.sum(w * g_ref[b], axis=1, keepdims=True)
        y_ref[b] = y
        panel = dot6(w, a_ref[lo:hi, lo:], NN)
        for c in range(b + 1, 4):
            off = c * NB - lo
            piece = panel[:, off:off + NB]
            a_ref[c * NB:(c + 1) * NB, c * NB:] -= dot6(piece, panel[:, off:], TN)
            g_ref[c] = g_ref[c] - jnp.sum(piece * y, axis=0, keepdims=True)
        r_ref[lo:hi, lo:hi] = jnp.where(upper, panel[:, :NB], 0.0)
        if b < 3:
            r_ref[lo:hi, hi:] = panel[:, NB:]
        put(b).start()
    xs = [None] * 4
    for b in reversed(range(4)):
        z = y_ref[b]
        if b < 3:
            d = r_ref[b * NB:(b + 1) * NB, (b + 1) * NB:(b + 2) * NB] * xs[b + 1]
            for c in range(b + 2, 4):
                d = d + r_ref[b * NB:(b + 1) * NB, c * NB:(c + 1) * NB] * xs[c]
            z = z - jnp.sum(d, axis=1, keepdims=True)
        xs[b] = jnp.sum(w_ref[b] * z, axis=0, keepdims=True)
    step_row = -jnp.concatenate(xs, axis=1)
    basis, chans = theta_ref.shape
    own = (iota((basis, PARAMS), 1) & 7) == iota((basis, PARAMS), 0)
    pick = ((iota((PARAMS, chans), 0) >> 3) == iota((PARAMS, chans), 1)).astype(jnp.bfloat16)
    rows = [jnp.where(own, t, 0.0).astype(jnp.bfloat16) for t in parts(step_row)]
    three = lax.dot_general(
        jnp.concatenate(rows[::-1], axis=0), pick, NN, preferred_element_type=F32)
    step = three[:basis] + three[basis:2 * basis] + three[2 * basis:]
    theta_out[...] = theta_ref[...] + step
    moved = dot(step, phi_ref[...], TN)
    pred = resid_ref[...] + jnp.sum(slope_ref[...] * moved, axis=0, keepdims=True)
    pred_ref[...] = jnp.concatenate([pred[:, :NB], pred[:, NB:]], axis=0)
    for b in range(4):
        put(b).wait()


THETA_T = True
VM = pl.BlockSpec(memory_space=pltpu.VMEM)


def sds(*shape):
    return jax.ShapeDtypeStruct(shape, F32)


def reduce_call(ysize, *args):
    basis, chans = args[5].shape
    slots = 256
    dma = pltpu.SemaphoreType.DMA
    four, grid, line = dma((QUARTERS,)), dma((QUARTERS, PLANE)), dma((ZN,))
    return pl.pallas_call(
        functools.partial(reduce_kernel, ysize),
        name="reduce",
        out_shape=tuple(pltpu.VMEM(d, F32) for d in ((ROWS + EXTRA, NB), (chans, slots), (basis, slots), (1, slots), (basis, chans))),
        in_specs=[pl.BlockSpec(memory_space=pl.ANY)] * 8,
        out_specs=(VM,) * 5,
        scratch_shapes=[pltpu.VMEM(a.shape, a.dtype) for a in args] + [
            dma((8,)),
            pltpu.VMEM((ROWS, NB), F32),
            pltpu.VMEM((QUARTERS, NB, NB), F32),
            pltpu.VMEM((QUARTERS, NB, NB), F32),
            pltpu.VMEM((QUARTERS, PLANE, 8, NB), F32),
            pltpu.VMEM((ZN, 2, NB), F32),
            pltpu.VMEM((ZN, 2, NB), F32),
            pltpu.VMEM((ZN, 2, NB), F32),
            pltpu.VMEM((ROWS, NB), F32),
            pltpu.VMEM((2, 8, NB), F32),
            pltpu.VMEM((PLANE, 8, NB), F32),
            pltpu.VMEM((ZN, 8, NB), F32),
        ] + [four] * 2 + [grid] * 2 + [line] * 4 + [grid] * 2 + [four] * 2 + [dma] * 2 + [line] * 4,
        compiler_params=pltpu.CompilerParams(collective_id=0, has_side_effects=True),
    )(*args)


def solve_call(summed, slope, phi, resid, theta):
    slots = resid.shape[1]
    return pl.pallas_call(
        solve_kernel,
        name="solve",
        out_shape=(sds(PARAMS, PARAMS), sds(*theta.shape), sds(slots // NB, NB)),
        in_specs=[VM] * 5,
        out_specs=(pl.BlockSpec(memory_space=pl.ANY), VM, VM),
        scratch_shapes=[
            pltpu.VMEM((PARAMS, PARAMS), F32),
            pltpu.VMEM((PARAMS, PARAMS), F32),
            pltpu.VMEM((4, NB, NB), F32),
            pltpu.VMEM((4, 1, NB), F32),
            pltpu.VMEM((4, NB, 1), F32),
            pltpu.SemaphoreType.DMA((4,)),
        ],
        compiler_params=pltpu.CompilerParams(vmem_limit_bytes=24 << 20),
    )(summed, slope, phi, resid, theta)


def on_device(images, gauge_pixel, row_mask, gauge_counts, targets, theta, amplitude, damping):
    def lanes(v):
        return v.reshape(-1, NB)

    terms = reduce_call(
        4, gauge_counts.reshape(1, 1), images.reshape(-1, NB), lanes(gauge_pixel), lanes(row_mask),
        lanes(targets), theta.T, amplitude.reshape(1, -1), damping.reshape(1, 1))
    r, new_theta, pred = solve_call(*terms)
    return r, new_theta.T, pred.reshape(-1)


def solution(mesh):
    return jax.shard_map(
        on_device,
        mesh=mesh,
        in_specs=(P("rows", None, None), P("rows"), P("rows"), P("rows"), P("rows"), P(), P(), P()),
        out_specs=(P(), P(), P(("rows", "cols"))),
        check_vma=False,
    )
```
